128 devices in a mesh: row: 8 (over x_hi, y), col: 16 (over z, x_lo, core).
Axes of the slice: x: 4 (x_hi: 2, x_lo: 2; x = x_hi * 2 + x_lo), y: 4, z: 4, core: 2. Of those that a mesh axis runs over, the one named last changes fastest.
Arguments:
- tokens: bfloat16 [16384, 2880], P(('col', 'row')), may hold values from -6 to 6
- seg_ids: int32 [16384], P(('col', 'row')), may hold values from 0 to 15, never falling along the last dimension, each value on 1 to 2048 neighbouring positions
- norm_gain: float32 [2880], replicated, may hold values from 0.1 to 1.9
- query_weight: bfloat16 [2880, 4096], P('col', 'row'), may hold values from -4.5839394 to 4.5839394
- kv_weight: bfloat16 [2880, 1024], P('col', 'row'), may hold values from -0.1118034 to 0.1118034
- out_weight: bfloat16 [4096, 2880], P('row', 'col'), may hold values from -0.09375 to 0.09375
- sinks: float32 [64], P('row'), may hold values from 1 to 6
- moe_gain: float32 [2880], replicated, may hold values from 0.1 to 1.9
- routes: int32 [16384, 4], P(('col', 'row')), may hold values from 0 to 63, all different within a row; in each aligned block of 128 rows (0 to 127, 128 to 255, ...) at most 9 rows name the same one
- route_weights: float32 [16384, 4], P(('col', 'row')), may hold values from 0.05 to 0.5
- expert_in: bfloat16 [128, 2880, 1536], P(('row', 'col')), may hold values from -0.109375 to 0.109375
- expert_out: bfloat16 [128, 768, 2880], P(('row', 'col')), may hold values from -0.21875 to 0.21875
Outputs:
- mixed: bfloat16 [16384, 2880], P(('col', 'row'))
- kv_cache: bfloat16 [16384, 1024], P('col', 'row')
The draws below stay inside these ranges and needn't reach their ends.
Inputs may be any that keep to these rules, and one draw needn't show every extreme that they name: `seg_ids`: never falling; each prompt has 1 to 2048 tokens, one exactly 2048. `routes`: each row names 4 different experts; among the 128 rows of one device no expert is named more than 9 times, and on some device one is named exactly 9 times.
All inputs are finite; a program needn't handle non-finite values.
Results may differ from the reference program's by a relative error of at most 0.012.
Values may be sent and summed in bfloat16 or wider, within the bound.
A program may use at most 128 MiB of HBM per device.

```python
import math
import jax
import jax.numpy as jnp
import numpy as np
from jax import lax

D = 2880
HQ = 64
KVH = 8
HD = 64
WIN = 128
EXPERTS = 64
HALF = 768
TOP = 4
TOK_DEV = 128
CAP = 9
TOKENS = 16384
MAXLEN = 2048
SEGS = 16
N_ROW = 8
N_COL = 16


strength_list = (12.0, 24.0, 40.0)


def key_value_block(key):
    entries = jax.random.normal(jax.random.fold_in(key, 101), (D, KVH, 2, HD), jnp.float32)
    entries = jnp.clip(entries, -6.0, 6.0) * D ** (-0.5)
    return entries


def draw_kv_weight(key, part):
    return key_value_block(key).reshape(D, KVH * 2 * HD).astype(jnp.bfloat16)


def draw_query_weight(key, part):
    key_columns = key_value_block(key)[:, :, 0, :]
    per_head = jnp.repeat(key_columns, HQ // KVH, axis=1)
    spread_part = jnp.clip(jax.random.normal(jax.random.fold_in(key, 102), (D, HQ, HD), jnp.float32), -6.0, 6.0) * D ** (-0.5)
    head_order = jax.random.permutation(jax.random.fold_in(key, 103), HQ)
    strengths = jnp.zeros((HQ,), jnp.float32).at[head_order[:3]].set(jnp.array(strength_list, jnp.float32))
    turning = (jnp.arange(HD, dtype=jnp.int32) % (HD // 2) != 0).astype(jnp.float32)
    lifted = strengths[:, None] * turning[None, :]
    return (spread_part + lifted[None] * per_head).reshape(D, HQ * HD).astype(jnp.bfloat16)


def draw_tokens(key, part):
    base_rows = jnp.clip(jax.random.normal(jax.random.fold_in(key, 201), (TOKENS, D), jnp.float32), -6.0, 6.0)
    leading = base_rows[0::2]
    trailing = base_rows[1::2]
    kept_width = D - D // 4
    mirrored = jnp.concatenate([leading[:, :kept_width], jnp.flip(leading[:, kept_width:], axis=1)], axis=1)
    picked = jax.random.randint(jax.random.fold_in(key, 202), (TOKENS // 2, 1), 0, 8) == 0
    trailing = jnp.where(picked, mirrored, trailing)
    return jnp.stack([leading, trailing], axis=1).reshape(TOKENS, D).astype(jnp.bfloat16)


def shard_levels(rng, extent, cuts, least, largest):
    gain = 1.0
    for axis_at, shards_of in cuts:
        steps = jax.random.uniform(jax.random.fold_in(jax.random.fold_in(rng, 6), axis_at), (shards_of,), jnp.float32, least / len(cuts), largest / len(cuts))
        gain = gain * jnp.repeat(jnp.exp(steps), extent[axis_at] // shards_of).reshape((-1,) + (1,) * (len(extent) - 1 - axis_at))
    return gain


def profile(count, total, limit, lean):
    weights = [(1 << 20) // math.isqrt(rank ** lean) + 1 for rank in range(2, count + 1)]
    spare, given = total - limit - (count - 1), [1] * (count - 1)
    while spare > 0:
        candidates = [i for i in range(count - 1) if given[i] < limit]
        mass, budget = sum([weights[i] for i in candidates]), spare
        for i in candidates:
            extra = min(limit - given[i], max(1, budget * weights[i] // mass), spare)
            given[i] = given[i] + extra
            spare = spare - extra
    return np.array([limit] + given)


def uneven_parts(own_key, number_of, total, most, slope):
    if number_of == 2:
        one = jax.random.randint(own_key, (), max(1, total - most), min(most, total - 1) + 1)
        return jnp.stack([one, total - one])
    lengths = jnp.asarray(profile(number_of, total, most, slope), jnp.int32)
    couples = (number_of - 1) // 2
    source_of, taker = lengths[1:1 + 2 * couples:2], lengths[2:2 + 2 * couples:2]
    room = jnp.minimum(source_of - 1, most - taker)
    passed = jax.random.randint(jax.random.fold_in(own_key, 1), (couples,), 0, 1 << 20) % (room + 1)
    lengths = lengths.at[1:1 + 2 * couples:2].set(source_of - passed).at[2:2 + 2 * couples:2].set(taker + passed)
    return lengths[jax.random.permutation(jax.random.fold_in(own_key, 2), number_of)]


def deal_out(key, own, number, rows, amount, top, reach, lean):
    order = jax.random.permutation(key, amount)
    crowded, common = shares(amount, rows * top, reach, lean, True), shares(amount, rows * top, reach, lean, False)
    places = jnp.arange(amount)

    def named(sizes, turn):
        used = int((sizes > 0).sum())
        fixed = max(1, used // 4)
        shifted = fixed + (places - fixed + turn * (used - fixed)) % max(1, amount - fixed)
        return jnp.zeros((amount,), jnp.int32).at[order[jnp.where(places < fixed, places, shifted)]].set(jnp.asarray(sizes, jnp.int32))

    sizes = jnp.where(number % 4 == 0, named(crowded, number // 4), named(common, number - number // 4 - 1))
    mixed = jax.random.permutation(jax.random.fold_in(own, 3), amount)
    giver, receiver = mixed[0:amount // 2 * 2:2], mixed[1:amount // 2 * 2:2]
    slack = jnp.minimum(sizes[giver] - 1, reach - sizes[receiver]) // 2
    slack = jnp.where((giver == order[0]) | (receiver == order[0]) | (sizes[receiver] == 0), 0, jnp.maximum(slack, 0))
    shifted = jax.random.randint(jax.random.fold_in(own, 4), (amount // 2,), 0, 1 << 20) % (slack + 1)
    sizes = sizes.at[giver].add(-shifted).at[receiver].add(shifted)
    items = jnp.searchsorted(jnp.cumsum(sizes), jnp.arange(rows * top), side="right").astype(jnp.int32)
    grid = items.reshape(top, rows).T
    grid = grid[jax.random.permutation(jax.random.fold_in(own, 1), rows)]
    turn = jax.random.randint(jax.random.fold_in(own, 2), (rows, 1), 0, top)
    return jnp.take_along_axis(grid, (jnp.arange(top)[None, :] + turn) % top, axis=1)


def shares(amount, total, reach, lean, full):
    loads = [(1 << 20) // math.isqrt(grade ** lean) + 1 for grade in range(1, amount + 1)]
    largest = reach if full else min(reach, max(-(-total // amount), total * loads[0] // sum(loads)))
    least = 1 if total - largest >= amount - 1 else 0
    given, rest = [largest] + [least] * (amount - 1), total - largest - least * (amount - 1)
    while rest > 0:
        free = [i for i in range(1, amount) if given[i] < largest] or [i for i in range(1, amount) if given[i] < reach]
        mass, left = sum([loads[i] for i in free]), rest
        for i in free:
            more = min(reach - given[i], max(1, left * loads[i] // mass), rest)
            given[i] = given[i] + more
            rest = rest - more
    return np.array(given)


def scatter_about(key, dims, spread, bound, cuts=(), kind=jnp.bfloat16):
    values = spread * jax.random.normal(key, dims, jnp.float32)
    if cuts:
        values = values * shard_levels(key, dims, cuts, -0.22, 0.18)
    return jnp.clip(values, -bound, bound).astype(kind)


def setup_inputs(seed: int = 0) -> dict:
    key_list = jax.random.split(jax.random.key(seed), 13)
    tokens = draw_tokens(jax.random.fold_in(key_list[12], 71), 0)
    seg_ids = jnp.searchsorted(jnp.cumsum(uneven_parts(key_list[1], SEGS, TOKENS, MAXLEN, 2)), jnp.arange(TOKENS), side="right").astype(jnp.int32)
    norm_gain = jnp.clip(1.0 + 0.18 * jax.random.normal(key_list[2], (D,), jnp.float32), 0.1, 1.9)
    query_weight = draw_query_weight(jax.random.fold_in(key_list[12], 71), 0)
    kv_weight = draw_kv_weight(jax.random.fold_in(key_list[12], 71), 0)
    out_weight = scatter_about(key_list[5], (HQ * HD, D), (HQ * HD) ** -0.5, 0.09375, ((0, 8), (1, 16)))
    sinks = jnp.clip(1.0 + 5.0 * jax.random.uniform(key_list[6], (HQ,), jnp.float32) ** shard_levels(key_list[6], (HQ,), ((0, 8),), -0.2, 0.2), 1.0, 6.0)
    moe_gain = jnp.clip(1.0 + 0.18 * jax.random.normal(key_list[7], (D,), jnp.float32), 0.1, 1.9)
    routes_keys = jax.random.split(jax.random.fold_in(key_list[8], 1), TOKENS // TOK_DEV)
    routes_turns = jax.random.permutation(jax.random.fold_in(key_list[8], 3), TOKENS // TOK_DEV)
    routes = jax.vmap(lambda own, number: deal_out(jax.random.fold_in(key_list[8], 2), own, number, TOK_DEV, EXPERTS, TOP, CAP, 1))(routes_keys, routes_turns).reshape((TOKENS, TOP))
    route_weights = jnp.clip(0.05 + 0.45 * jax.random.uniform(key_list[9], (TOKENS, TOP), jnp.float32) ** shard_levels(key_list[9], (TOKENS, TOP), ((0, 128),), -0.2, 0.2), 0.05, 0.5)
    expert_in = scatter_about(key_list[10], (2 * EXPERTS, D, 2 * HALF), D ** -0.5, 0.109375, ((0, 128),))
    expert_out = scatter_about(key_list[11], (2 * EXPERTS, HALF, D), HALF ** -0.5, 0.21875, ((0, 128),))
    return {"tokens": tokens, "seg_ids": seg_ids, "norm_gain": norm_gain, "query_weight": query_weight, "kv_weight": kv_weight, "out_weight": out_weight, "sinks": sinks, "moe_gain": moe_gain, "routes": routes, "route_weights": route_weights, "expert_in": expert_in, "expert_out": expert_out}


eps_norm = 1e-05
theta_base = 150000.0
glu_alpha = 1.702
masked_score = -1e+30

def rms_scale(values_in, gain_vec):
    widened = values_in.astype(jnp.float32)
    return widened * lax.rsqrt(lax.optimization_barrier(jnp.mean(widened * widened, axis=-1, keepdims=True)) + eps_norm) * gain_vec

def rotate(values_in, positions):
    half_dim = values_in.shape[-1] // 2
    frequency = jnp.exp(jnp.arange(half_dim, dtype=jnp.float32) * (-2.0 * math.log(theta_base) / values_in.shape[-1]))
    angles = positions.astype(jnp.float32)[:, None] * frequency[None, :]
    cosine = jnp.cos(angles)[:, None, :]
    sine = jnp.sin(angles)[:, None, :]
    first_half = values_in[..., :half_dim]
    second_half = values_in[..., half_dim:]
    return jnp.concatenate([first_half * cosine - second_half * sine, second_half * cosine + first_half * sine], axis=-1)

def run_positions(segments):
    count_all = segments.shape[0]
    index_all = jnp.arange(count_all, dtype=jnp.int32)
    before = jnp.concatenate([jnp.full((1,), -1, jnp.int32), segments[:-1]])
    marks = jnp.where(segments != before, index_all, jnp.int32(0))
    return index_all - lax.cummax(marks)

def attend_tile(query_tile, key_tile, value_tile, query_seg, key_seg, query_pos, key_pos, sink_grid):
    scores = jnp.einsum('qkgd,lkd->kgql', query_tile, key_tile) * query_tile.shape[-1] ** (-0.5)
    distance = query_pos[:, None] - key_pos[None, :]
    allowed = (query_seg[:, None] == key_seg[None, :]) & (distance >= 0) & (distance < WIN) & (key_pos[None, :] >= 0)
    scores = jnp.where(allowed[None, None], scores, masked_score)
    sink_col = sink_grid[:, :, None]
    ceiling = jnp.maximum(lax.optimization_barrier(jnp.max(scores, axis=-1)), sink_col)
    expo = jnp.exp(scores - ceiling[..., None])
    denom = lax.optimization_barrier(jnp.sum(expo, axis=-1)) + jnp.exp(sink_col - ceiling)
    probs = (expo / denom[..., None]).astype(jnp.bfloat16)
    return jnp.einsum('kgql,lkd->qkgd', probs.astype(jnp.float32), value_tile).astype(jnp.bfloat16)

def attention_all(queries, keys, values, segments, sinks):
    group_size = HQ // KVH
    query_grid = queries.reshape(TOKENS // WIN, WIN, KVH, group_size, HD)
    key_padded = jnp.concatenate([jnp.zeros((WIN, KVH, HD), jnp.bfloat16), keys])
    value_padded = jnp.concatenate([jnp.zeros((WIN, KVH, HD), jnp.bfloat16), values])
    seg_padded = jnp.concatenate([jnp.full((WIN,), -1, jnp.int32), segments])
    sink_grid = sinks.reshape(KVH, group_size)

    def one_block(block_id):
        first_row = block_id * WIN
        query_tile = lax.dynamic_index_in_dim(query_grid, block_id, 0, keepdims=False).astype(jnp.float32)
        key_tile = lax.dynamic_slice_in_dim(key_padded, first_row, 2 * WIN, 0).astype(jnp.float32)
        value_tile = lax.dynamic_slice_in_dim(value_padded, first_row, 2 * WIN, 0).astype(jnp.float32)
        key_seg = lax.dynamic_slice_in_dim(seg_padded, first_row, 2 * WIN, 0)
        query_seg = lax.dynamic_slice_in_dim(segments, first_row, WIN, 0)
        query_pos = first_row + jnp.arange(WIN, dtype=jnp.int32)
        key_pos = first_row - WIN + jnp.arange(2 * WIN, dtype=jnp.int32)
        return attend_tile(query_tile, key_tile, value_tile, query_seg, key_seg, query_pos, key_pos, sink_grid)
    tiles = lax.map(one_block, jnp.arange(TOKENS // WIN, dtype=jnp.int32))
    return tiles.reshape(TOKENS, HQ * HD)

def experts_all(moe_in, routes, route_weights, expert_in, expert_out):
    route_flat = routes.reshape(-1)
    weight_flat = route_weights.reshape(-1)
    total_routes = route_flat.shape[0]
    ordering = jnp.argsort(route_flat, stable=True).astype(jnp.int32)
    expert_ids = jnp.arange(EXPERTS, dtype=jnp.int32)
    counts = lax.optimization_barrier(jnp.sum((route_flat[:, None] == expert_ids[None, :]).astype(jnp.int32), axis=0))
    offsets = jnp.cumsum(counts) - counts
    most_rows = N_ROW * N_COL * CAP

    def one_expert(running, expert):
        places = offsets[expert] + jnp.arange(most_rows, dtype=jnp.int32)
        valid = jnp.arange(most_rows, dtype=jnp.int32) < counts[expert]
        chosen = ordering[jnp.minimum(places, total_routes - 1)]
        token_ids = chosen // TOP
        rows_in = moe_in[token_ids]
        summed = jnp.zeros((most_rows, D), jnp.float32)
        for half_id in range(2):
            slice_id = 2 * expert + half_id
            mixed_in = jnp.dot(rows_in, expert_in[slice_id], preferred_element_type=jnp.float32)
            gate_part = mixed_in[:, :HALF]
            up_part = mixed_in[:, HALF:]
            hidden_act = (gate_part * jax.nn.sigmoid(glu_alpha * gate_part) * (up_part + 1.0)).astype(jnp.bfloat16)
            part_out = jnp.dot(hidden_act, expert_out[slice_id], preferred_element_type=jnp.float32).astype(jnp.bfloat16)
            part_out = lax.optimization_barrier(part_out)
            summed = summed + part_out.astype(jnp.float32)
        scaled = jnp.where(valid, weight_flat[chosen], jnp.float32(0.0))
        running = running.at[token_ids].add(scaled[:, None] * summed)
        return (running, None)
    result, _ = lax.scan(one_expert, jnp.zeros((TOKENS, D), jnp.float32), expert_ids)
    return result

def reference(tokens, seg_ids, norm_gain, query_weight, kv_weight, out_weight, sinks, moe_gain, routes, route_weights, expert_in, expert_out):
    normed = rms_scale(tokens, norm_gain).astype(jnp.bfloat16)
    positions = run_positions(seg_ids)
    query_raw = jnp.dot(normed, query_weight, preferred_element_type=jnp.float32).reshape(TOKENS, HQ, HD)
    queries = rotate(query_raw, positions).astype(jnp.bfloat16)
    kv_raw = jnp.dot(normed, kv_weight, preferred_element_type=jnp.float32).reshape(TOKENS, KVH, 2, HD)
    keys = rotate(kv_raw[:, :, 0], positions).astype(jnp.bfloat16)
    values = kv_raw[:, :, 1].astype(jnp.bfloat16)
    kv_cache = jnp.stack([keys, values], axis=2).reshape(TOKENS, KVH * 2 * HD)
    attended = attention_all(queries, keys, values, seg_ids, sinks)
    group_cols = HQ * HD // N_ROW
    hidden = tokens.astype(jnp.float32)
    for group_id in range(N_ROW):
        partial_value = jnp.dot(attended[:, group_id * group_cols:(group_id + 1) * group_cols], out_weight[group_id * group_cols:(group_id + 1) * group_cols], preferred_element_type=jnp.float32).astype(jnp.bfloat16)
        partial_value = lax.optimization_barrier(partial_value)
        hidden = hidden + partial_value.astype(jnp.float32)
    moe_in = rms_scale(hidden, moe_gain).astype(jnp.bfloat16)
    mixed = (hidden + experts_all(moe_in, routes, route_weights, expert_in, expert_out)).astype(jnp.bfloat16)
    return (mixed, kv_cache)
```

```python
import math

import jax
import jax.numpy as jnp
from jax import lax
from jax.experimental import pallas as pl
from jax.experimental.pallas import tpu as pltpu
from jax.sharding import PartitionSpec as P

HD = 64
WIN = 128
EXPERTS = 64
TOP = 4
CAP = 9


eps_norm = 1e-05
theta_base = 150000.0
glu_alpha = 1.702
masked_score = -1e30


def entering(part, axis, combine, identity):
    place = lax.axis_index(axis)
    gathered = jax.tree.map(lambda a: lax.all_gather(a, axis), part)
    state = jax.tree.map(lambda a, e: jnp.zeros_like(a) + jnp.asarray(e, a.dtype), part, identity)

    def one(step, state):
        return combine(
            state, jax.tree.map(lambda a: lax.dynamic_index_in_dim(a, step, 0, False), gathered)
        )

    return lax.fori_loop(0, place, one, state)


def from_behind(value, axis, steps):
    count = lax.axis_size(axis)
    first, last = (max(0, -steps), min(count, count - steps))
    return lax.ppermute(value, axis, [(source, source + steps) for source in range(first, last)])


def rms_scale(values_in, gain_vec):
    widened = values_in.astype(jnp.float32)
    return (
        widened
        * lax.rsqrt(jnp.mean(widened * widened, axis=-1, keepdims=True) + eps_norm)
        * gain_vec
    )


def rotate(values_in, positions):
    half_dim = values_in.shape[-1] // 2
    frequency = jnp.exp(
        jnp.arange(half_dim, dtype=jnp.float32)
        * (-2.0 * math.log(theta_base) / values_in.shape[-1])
    )
    angles = positions.astype(jnp.float32)[:, None] * frequency[None, :]
    cosine = jnp.cos(angles)[:, None, :]
    sine = jnp.sin(angles)[:, None, :]
    first_half = values_in[..., :half_dim]
    second_half = values_in[..., half_dim:]
    return jnp.concatenate(
        [first_half * cosine - second_half * sine, second_half * cosine + first_half * sine],
        axis=-1,
    )


def joined(earlier, later):
    first_early, last_early, start_early = earlier
    first_late, last_late, start_late = later
    first_seg = jnp.where(first_early < 0, first_late, first_early)
    last_seg = jnp.where(last_late < 0, last_early, last_late)
    carried = (first_late == last_late) & (last_early == first_late) | (first_late < 0)
    return (first_seg, last_seg, jnp.where(carried, start_early, start_late))


def attend_tile(
    query_tile, key_tile, value_tile, query_seg, key_seg, query_pos, key_pos, sink_grid
):
    scores = jnp.einsum(
        "qkgd,lkd->kgql", query_tile, key_tile, preferred_element_type=jnp.float32
    ) * query_tile.shape[-1] ** (-0.5)
    distance = query_pos[:, None] - key_pos[None, :]
    allowed = (
        (query_seg[:, None] == key_seg[None, :])
        & (distance >= 0)
        & (distance < WIN)
        & (key_pos[None, :] >= 0)
    )
    scores = jnp.where(allowed[None, None], scores, masked_score)
    sink_col = sink_grid[:, :, None]
    ceiling = jnp.maximum(jnp.max(scores, axis=-1), sink_col)
    expo = jnp.exp(scores - ceiling[..., None])
    denom = jnp.sum(expo, axis=-1) + jnp.exp(sink_col - ceiling)
    probs = (expo / denom[..., None]).astype(jnp.bfloat16)
    return jnp.einsum(
        "kgql,lkd->qkgd", probs, value_tile, preferred_element_type=jnp.float32
    ).astype(jnp.bfloat16)


def chip_place():
    row, col = lax.axis_index("row"), lax.axis_index("col")
    return (row // 4) * 2 + (col // 2) % 2, row % 4, col // 4, col % 2


def device_at(x, y, z, core):
    return ((x // 2) * 4 + y, z * 4 + (x % 2) * 2 + core)


def expert_at(x, y, z):
    return ((x // 2) * 4 + y) * 8 + z * 2 + x % 2


def hop_order():
    every = [(a, b, c) for a in range(4) for b in range(4) for c in range(4)]
    reach = lambda v: sum(min(s, 4 - s) for s in v)
    return sorted([v for v in every if v != (0, 0, 0)], key=lambda v: -reach(v))


def exchange_kernel(out_msgs, in_msgs, send_sem, recv_sem, own_sem):
    x, y, z, core = chip_place()
    me = expert_at(x, y, z)
    offsets = hop_order()
    barrier = pltpu.get_barrier_semaphore()
    for dx, dy, dz in offsets:
        pl.semaphore_signal(
            barrier,
            inc=1,
            device_id=device_at((x + dx) % 4, (y + dy) % 4, (z + dz) % 4, core),
            device_id_type=pl.DeviceIdType.MESH,
        )
    own = pltpu.make_async_copy(out_msgs.at[me], in_msgs.at[me], own_sem)
    own.start()
    pl.semaphore_wait(barrier, len(offsets))
    copies = []
    for number, (dx, dy, dz) in enumerate(offsets):
        there = ((x + dx) % 4, (y + dy) % 4, (z + dz) % 4)
        copy = pltpu.make_async_remote_copy(
            src_ref=out_msgs.at[expert_at(*there)],
            dst_ref=in_msgs.at[me],
            send_sem=send_sem.at[number],
            recv_sem=recv_sem.at[number],
            device_id=device_at(*there, core),
            device_id_type=pl.DeviceIdType.MESH,
        )
        copy.start()
        copies.append(copy)
    own.wait()
    for copy in copies:
        copy.wait()


def exchange(messages, ident, name):
    others = EXPERTS - 1
    return pl.pallas_call(
        exchange_kernel,
        out_shape=jax.ShapeDtypeStruct(messages.shape, messages.dtype),
        in_specs=[pl.BlockSpec(memory_space=pl.ANY)],
        out_specs=pl.BlockSpec(memory_space=pl.ANY),
        scratch_shapes=[
            pltpu.SemaphoreType.DMA((others,)),
            pltpu.SemaphoreType.DMA((others,)),
            pltpu.SemaphoreType.DMA,
        ],
        compiler_params=pltpu.CompilerParams(collective_id=ident, has_side_effects=True),
        name=name,
    )(messages)


def slot_grid(routes_t, tokens_here):
    expert_ids = lax.broadcasted_iota(jnp.int32, (EXPERTS, tokens_here), 0)
    hit = jnp.zeros((EXPERTS, tokens_here), jnp.float32)
    for j in range(TOP):
        hit = hit + (routes_t[j : j + 1, :] == expert_ids).astype(jnp.float32)
    earlier = (
        lax.broadcasted_iota(jnp.int32, (tokens_here, tokens_here), 0)
        < lax.broadcasted_iota(jnp.int32, (tokens_here, tokens_here), 1)
    ).astype(jnp.bfloat16)
    rank = jnp.dot(hit.astype(jnp.bfloat16), earlier, preferred_element_type=jnp.float32)
    return hit, rank


def by_slot(hit, rank, amount):
    tokens_here = hit.shape[1]
    slot_ids = lax.broadcasted_iota(jnp.int32, (EXPERTS, 8, tokens_here), 1).astype(jnp.float32)
    first = jnp.where(
        (hit[:, None, :] > 0.5) & (rank[:, None, :] == slot_ids), amount[:, None, :], 0.0
    ).reshape(EXPERTS * 8, tokens_here)
    last = jnp.where((hit > 0.5) & (rank == 8.0), amount, 0.0)
    return first, last


def tiles_of(width):
    return [(k, k * 128, min(128, width - k * 128)) for k in range(-(-width // 128))]


def widen(tile):
    short = 128 - tile.shape[1]
    if short:
        tile = jnp.concatenate([tile, jnp.zeros((tile.shape[0], short), tile.dtype)], axis=1)
    return tile


def pack_message(out_ref, last_ref, tile_first, tile_last, k):
    out_ref[:, k] = widen(tile_first).reshape(EXPERTS, 8, 128).astype(jnp.bfloat16)
    last_ref[pl.ds(k, EXPERTS, stride=24), :] = widen(tile_last)


def finish_message(out_ref, last_ref, tile_count):
    for k in range(tile_count, 24):
        last_ref[pl.ds(k, EXPERTS, stride=24), :] = jnp.zeros((EXPERTS, 128), jnp.float32)
    out_ref[:, tile_count:] = (
        last_ref[...].reshape(EXPERTS, 3, 8, 128).astype(jnp.bfloat16)
    )


def unpack_last(in_ref, last_ref, tile_count):
    last_ref[...] = in_ref[:, tile_count:].astype(jnp.float32).reshape(EXPERTS * 24, 128)


def unpack_tile(in_ref, last_ref, k):
    first = in_ref[:, k].astype(jnp.float32).reshape(EXPERTS * 8, 128)
    last = last_ref[pl.ds(k, EXPERTS, stride=24), :]
    return jnp.concatenate([first, last], axis=0).astype(jnp.bfloat16)


def dispatch_kernel(tok_ref, add_ref, gain_ref, routes_ref, out_ref, last_ref):
    hidden = tok_ref[...].astype(jnp.float32) + add_ref[...].astype(jnp.float32)
    moe_in = rms_scale(hidden, gain_ref[...]).astype(jnp.bfloat16)
    hit, rank = slot_grid(routes_ref[...], hidden.shape[0])
    first, last = by_slot(hit, rank, jnp.ones_like(hit))
    first, last = first.astype(jnp.bfloat16), last.astype(jnp.bfloat16)
    tiles = tiles_of(hidden.shape[1])
    for k, start, width in tiles:
        piece = moe_in[:, start : start + width]
        pack_message(
            out_ref,
            last_ref,
            jnp.dot(first, piece, preferred_element_type=jnp.float32),
            jnp.dot(last, piece, preferred_element_type=jnp.float32),
            k,
        )
    finish_message(out_ref, last_ref, len(tiles))


def combine_kernel(tok_ref, add_ref, routes_ref, weights_ref, in_ref, out_ref, last_ref):
    routes_t, weights_t = routes_ref[...], weights_ref[...]
    tokens_here = routes_t.shape[1]
    hit, rank = slot_grid(routes_t, tokens_here)
    expert_ids = lax.broadcasted_iota(jnp.int32, (EXPERTS, tokens_here), 0)
    amount = jnp.zeros((EXPERTS, tokens_here), jnp.float32)
    for j in range(TOP):
        amount = amount + jnp.where(
            routes_t[j : j + 1, :] == expert_ids, weights_t[j : j + 1, :], 0.0
        )
    mix = jnp.concatenate(by_slot(hit, rank, amount), axis=0).T
    mix_high = mix.astype(jnp.bfloat16)
    mix_low = (mix - mix_high.astype(jnp.float32)).astype(jnp.bfloat16)
    tiles = tiles_of(out_ref.shape[1])
    unpack_last(in_ref, last_ref, len(tiles))
    for k, start, width in tiles:
        rows = unpack_tile(in_ref, last_ref, k)
        total = jnp.dot(mix_high, rows, preferred_element_type=jnp.float32) + jnp.dot(
            mix_low, rows, preferred_element_type=jnp.float32
        )
        here = slice(start, start + width)
        hidden = tok_ref[:, here].astype(jnp.float32) + add_ref[:, here].astype(jnp.float32)
        out_ref[:, here] = (hidden + total[:, :width]).astype(jnp.bfloat16)


def expert_kernel(
    in_ref, gate_a, up_a, down_a, gate_b, up_b, down_b, out_ref, rows_ref, total_ref, last_ref
):
    half, step = pl.program_id(0), pl.program_id(1)
    width = total_ref.shape[1]
    tiles = tiles_of(width)

    @pl.when((half == 0) & (step == 0))
    def _():
        unpack_last(in_ref, last_ref, len(tiles))
        for k, start, wide in tiles:
            rows_ref[:, start : start + wide] = unpack_tile(in_ref, last_ref, k)[:, :wide]

    def run(gate, up, down, fresh):
        rows = rows_ref[...]
        gate_part = jnp.dot(rows, gate[0], preferred_element_type=jnp.float32)
        up_part = jnp.dot(rows, up[0], preferred_element_type=jnp.float32)
        act = (gate_part * jax.nn.sigmoid(glu_alpha * gate_part) * (up_part + 1.0)).astype(
            jnp.bfloat16
        )
        part = lax.dot_general(
            act, down[0], (((1,), (1,)), ((), ())), preferred_element_type=jnp.float32
        )
        if fresh:
            total_ref[...] = part
        else:
            total_ref[...] += part

    @pl.when((half == 0) & (step == 0))
    def _():
        run(gate_a, up_a, down_a, True)

    @pl.when((half == 0) & (step != 0))
    def _():
        run(gate_a, up_a, down_a, False)

    @pl.when(half == 1)
    def _():
        run(gate_b, up_b, down_b, False)

    @pl.when((half == 1) & (step == pl.num_programs(1) - 1))
    def _():
        for k, start, wide in tiles:
            tile = total_ref[:, start : start + wide]
            pack_message(out_ref, last_ref, tile[: EXPERTS * 8], tile[EXPERTS * 8 :], k)
        finish_message(out_ref, last_ref, len(tiles))


def run_experts(arrived, own_in, own_out, peer_in, peer_out):
    width, half_width = own_in.shape[1], own_out.shape[2]
    chunk = 256
    steps = half_width // chunk
    first = lambda h, s: jnp.where(h == 0, s, steps - 1)
    second = lambda h, s: jnp.where(h == 0, 0, s)
    block_in, block_out = (1, width, chunk), (1, width, chunk)
    specs = []
    for pick in (first, second):
        specs += [
            pl.BlockSpec(block_in, lambda h, s, pick=pick: (0, 0, pick(h, s))),
            pl.BlockSpec(block_in, lambda h, s, pick=pick: (0, 0, pick(h, s) + steps)),
            pl.BlockSpec(block_out, lambda h, s, pick=pick: (0, 0, pick(h, s))),
        ]
    rows = EXPERTS * CAP
    return pl.pallas_call(
        expert_kernel,
        grid=(2, steps),
        out_shape=jax.ShapeDtypeStruct(arrived.shape, arrived.dtype),
        in_specs=[pl.BlockSpec(memory_space=pltpu.VMEM)] + specs,
        out_specs=pl.BlockSpec(memory_space=pltpu.VMEM),
        scratch_shapes=[
            pltpu.VMEM((rows, width), jnp.bfloat16),
            pltpu.VMEM((rows, width), jnp.float32),
            pltpu.VMEM((EXPERTS * 24, 128), jnp.float32),
        ],
        compiler_params=pltpu.CompilerParams(vmem_limit_bytes=60 * 2**20),
        name="experts",
    )(arrived, own_in, own_in, own_out, peer_in, peer_in, peer_out)


def expert_layer(tokens, head_total, moe_gain, routes, route_weights, own, peer):
    tokens_here, width = tokens.shape
    vmem = pl.BlockSpec(memory_space=pltpu.VMEM)
    message = jax.ShapeDtypeStruct((EXPERTS, -(-width // 128) + 3, 8, 128), jnp.bfloat16)
    last = pltpu.VMEM((EXPERTS * 24, 128), jnp.float32)
    outgoing = pl.pallas_call(
        dispatch_kernel,
        out_shape=message,
        in_specs=[vmem] * 4,
        out_specs=vmem,
        scratch_shapes=[last],
        compiler_params=pltpu.CompilerParams(vmem_limit_bytes=40 * 2**20),
        name="dispatch",
    )(tokens, head_total, moe_gain.reshape(1, width), routes.T)
    arrived = exchange(outgoing, 1, "exchange_out")
    produced = run_experts(arrived, *own, *peer)
    returned = exchange(produced, 2, "exchange_back")
    return pl.pallas_call(
        combine_kernel,
        out_shape=jax.ShapeDtypeStruct((tokens_here, width), jnp.bfloat16),
        in_specs=[vmem] * 5,
        out_specs=vmem,
        scratch_shapes=[last],
        compiler_params=pltpu.CompilerParams(vmem_limit_bytes=40 * 2**20),
        name="combine",
    )(tokens, head_total, routes.T, route_weights.T, returned)


def shards(
    tokens,
    seg_ids,
    norm_gain,
    query_weight,
    kv_weight,
    out_weight,
    sinks,
    moe_gain,
    routes,
    route_weights,
    expert_in,
    expert_out,
):
    swap = [(c, c + 1 - 2 * (c % 2)) for c in range(lax.axis_size("col"))]
    own_in, own_out = expert_in, jnp.swapaxes(expert_out, 1, 2)
    peer_in, peer_out = (lax.ppermute(w, "col", swap) for w in (own_in, own_out))
    normed = rms_scale(tokens, norm_gain).astype(jnp.bfloat16)
    block_x, block_seg = (
        lax.all_gather(normed, "row", axis=0, tiled=True),
        lax.all_gather(seg_ids, "row", axis=0, tiled=True),
    )
    block_rows = block_x.shape[0]
    base_index = lax.axis_index("col") * block_rows
    token_index = base_index + jnp.arange(block_rows, dtype=jnp.int32)
    before = jnp.concatenate([block_seg[:1], block_seg[:-1]])
    own_start = lax.cummax(jnp.where(block_seg != before, token_index, base_index))
    summary = (block_seg[0], block_seg[block_rows - 1], own_start[block_rows - 1])
    neutral = (jnp.int32(-1), jnp.int32(-1), jnp.int32(-1))
    prior = entering(summary, "col", joined, neutral)
    lead_start = jnp.where(prior[1] == block_seg[0], prior[2], base_index)
    positions = token_index - jnp.where(own_start == base_index, lead_start, own_start)
    query_cols = query_weight.shape[1]
    kv_cols = kv_weight.shape[1]
    query_sum = jnp.dot(
        block_x,
        lax.all_gather(query_weight, "col", axis=0, tiled=True),
        preferred_element_type=jnp.float32,
    )
    kv_sum = jnp.dot(
        block_x,
        lax.all_gather(kv_weight, "col", axis=0, tiled=True),
        preferred_element_type=jnp.float32,
    )
    query_heads = query_cols // HD
    kv_heads = kv_cols // (2 * HD)
    group_size = query_heads // kv_heads
    queries = rotate(query_sum.reshape(block_rows, query_heads, HD), positions).astype(jnp.bfloat16)
    kv_pair = kv_sum.reshape(block_rows, kv_heads, 2, HD)
    keys = rotate(kv_pair[:, :, 0], positions).astype(jnp.bfloat16)
    values = kv_pair[:, :, 1].astype(jnp.bfloat16)
    kv_cache = jnp.stack([keys, values], axis=2).reshape(block_rows, kv_cols)
    edge_kv, edge_seg = from_behind(
        (kv_cache[block_rows - WIN :], block_seg[block_rows - WIN :]), "col", 1
    )
    all_kv = jnp.concatenate([edge_kv, kv_cache], axis=0).reshape(WIN + block_rows, kv_heads, 2, HD)
    all_seg = jnp.concatenate([edge_seg, block_seg])
    key_index = base_index - WIN + jnp.arange(WIN + block_rows, dtype=jnp.int32)
    span_rows = math.gcd(block_rows, 512)
    query_grid = queries.reshape(block_rows // span_rows, span_rows, kv_heads, group_size, HD)
    sink_grid = sinks.reshape(kv_heads, group_size)

    def attend_step(step_id):
        first_row = step_id * span_rows
        query_tile = lax.dynamic_index_in_dim(query_grid, step_id, 0, keepdims=False)
        kv_tile = lax.dynamic_slice_in_dim(all_kv, first_row, span_rows + WIN, 0)
        key_seg = lax.dynamic_slice_in_dim(all_seg, first_row, span_rows + WIN, 0)
        key_pos = lax.dynamic_slice_in_dim(key_index, first_row, span_rows + WIN, 0)
        query_seg = lax.dynamic_slice_in_dim(block_seg, first_row, span_rows, 0)
        query_pos = lax.dynamic_slice_in_dim(token_index, first_row, span_rows, 0)
        tile_out = attend_tile(
            query_tile,
            kv_tile[:, :, 0],
            kv_tile[:, :, 1],
            query_seg,
            key_seg,
            query_pos,
            key_pos,
            sink_grid,
        )
        return tile_out.reshape(span_rows, query_cols)

    attended = lax.map(attend_step, jnp.arange(block_rows // span_rows, dtype=jnp.int32)).reshape(
        block_rows, query_cols
    )
    partial_value = jnp.dot(
        attended,
        lax.all_gather(out_weight, "col", axis=1, tiled=True),
        preferred_element_type=jnp.float32,
    )
    head_total = lax.psum_scatter(
        partial_value.astype(jnp.bfloat16), "row", scatter_dimension=0, tiled=True
    )
    mixed = expert_layer(
        tokens, head_total, moe_gain, routes, route_weights, (own_in, own_out), (peer_in, peer_out)
    )
    return (mixed, kv_cache)


def solution(mesh):
    in_specs = (
        P(("col", "row"), None),
        P(("col", "row")),
        P(),
        P("col", "row"),
        P("col", "row"),
        P("row", "col"),
        P("row"),
        P(),
        P(("col", "row"), None),
        P(("col", "row"), None),
        P(("row", "col"), None, None),
        P(("row", "col"), None, None),
    )
    out_specs = (P(("col", "row"), None), P("col", "row"))
    return jax.shard_map(shards, mesh=mesh, in_specs=in_specs, out_specs=out_specs, check_vma=False)
```

```python
import functools
import math

import jax
import jax.numpy as jnp
from jax import lax
from jax.experimental import pallas as pl
from jax.experimental.pallas import tpu as pltpu
from jax.sharding import PartitionSpec as P

HD = 64
WIN = 128
EXPERTS = 64
TOP = 4
CAP = 9
SEGS = 16


eps_norm = 1e-05
theta_base = 150000.0
glu_alpha = 1.702
masked_score = -1e30


def rms_scale(widened, gain_vec, width):
    mean_square = jnp.sum(widened * widened, axis=-1, keepdims=True) * (1.0 / width)
    return widened * lax.rsqrt(mean_square + eps_norm) * gain_vec


def chip_place():
    row, col = lax.axis_index("row"), lax.axis_index("col")
    return (row // 4) * 2 + (col // 2) % 2, row % 4, col // 4, col % 2


def device_at(x, y, z, core):
    return ((x // 2) * 4 + y, z * 4 + (x % 2) * 2 + core)


def expert_at(x, y, z):
    return ((x // 2) * 4 + y) * 8 + z * 2 + x % 2


def hop_order():
    every = [(a, b, c) for a in range(4) for b in range(4) for c in range(4)]
    reach = lambda v: sum(min(s, 4 - s) for s in v)
    return sorted([v for v in every if v != (0, 0, 0)], key=lambda v: -reach(v))


def exchange_kernel(out_msgs, in_msgs, send_sem, recv_sem, own_sem):
    x, y, z, core = chip_place()
    me = expert_at(x, y, z)
    offsets = hop_order()
    barrier = pltpu.get_barrier_semaphore()
    for dx, dy, dz in offsets:
        pl.semaphore_signal(
            barrier,
            inc=1,
            device_id=device_at((x + dx) % 4, (y + dy) % 4, (z + dz) % 4, core),
            device_id_type=pl.DeviceIdType.MESH,
        )
    own = pltpu.make_async_copy(out_msgs.at[me], in_msgs.at[me], own_sem)
    own.start()
    pl.semaphore_wait(barrier, len(offsets))
    copies = []
    for number, (dx, dy, dz) in enumerate(offsets):
        there = ((x + dx) % 4, (y + dy) % 4, (z + dz) % 4)
        copy = pltpu.make_async_remote_copy(
            src_ref=out_msgs.at[expert_at(*there)],
            dst_ref=in_msgs.at[me],
            send_sem=send_sem.at[number],
            recv_sem=recv_sem.at[number],
            device_id=device_at(*there, core),
            device_id_type=pl.DeviceIdType.MESH,
        )
        copy.start()
        copies.append(copy)
    own.wait()
    for copy in copies:
        copy.wait()


def exchange(messages, ident, name):
    others = EXPERTS - 1
    return pl.pallas_call(
        exchange_kernel,
        out_shape=jax.ShapeDtypeStruct(messages.shape, messages.dtype),
        in_specs=[pl.BlockSpec(memory_space=pl.ANY)],
        out_specs=pl.BlockSpec(memory_space=pl.ANY),
        scratch_shapes=[
            pltpu.SemaphoreType.DMA((others,)),
            pltpu.SemaphoreType.DMA((others,)),
            pltpu.SemaphoreType.DMA,
        ],
        compiler_params=pltpu.CompilerParams(collective_id=ident, has_side_effects=True),
        name=name,
    )(messages)


def send(source, target, sems, number, device):
    copy = pltpu.make_async_remote_copy(
        src_ref=source,
        dst_ref=target,
        send_sem=sems[0].at[number],
        recv_sem=sems[1].at[number],
        device_id=device,
        device_id_type=pl.DeviceIdType.MESH,
    )
    copy.start()
    return copy


def greet(devices):
    barrier = pltpu.get_barrier_semaphore()
    for device in devices:
        pl.semaphore_signal(
            barrier, inc=1, device_id=device, device_id_type=pl.DeviceIdType.MESH
        )
    pl.semaphore_wait(barrier, len(devices))


class Ring:
    def __init__(self, own, place, device, sems, first):
        self.place, self.device, self.sems, self.first = place, device, sems, first
        self.sent = [
            self.pass_on(0, own(0), 0, 0, 1),
            self.pass_on(1, own(1), 0, 1, 1),
            self.pass_on(2, own(1), 0, 1, 3),
            self.pass_on(3, own(0), 0, 0, 3),
        ]

    def pass_on(self, number, source, owner, half, to):
        return send(
            source, self.place(owner, half), self.sems, self.first + number, self.device(to)
        )

    def take_left(self):
        self.sent[0].wait_recv()
        self.sent.append(self.pass_on(4, self.place(3, 0), 3, 0, 1))
        self.sent[1].wait_recv()

    def take_right(self):
        self.sent[2].wait_recv()
        self.sent.append(self.pass_on(5, self.place(1, 1), 1, 1, 3))
        self.sent[3].wait_recv()

    def take_far(self):
        self.sent[4].wait_recv()
        self.sent[5].wait_recv()

    def close(self):
        for copy in self.sent:
            copy.wait_send()


SHARD_CUT = 96


def gather_kernel(
    width,
    xt_ref,
    gain_ref,
    seg_ref,
    freq_ref,
    shard_ref,
    x_all,
    w_all,
    cos_ref,
    sin_ref,
    pos_ref,
    normed_ref,
    window_ref,
    send_sem,
    recv_sem,
    own_sem,
):
    x, y, z, core = chip_place()
    sems = (send_sem, recv_sem)
    run = lax.axis_index("col") * 2 + x // 2
    runs = 2 * lax.axis_size("col")
    shard_rows, shard_cols = shard_ref.shape

    def at(first, second):
        return (
            (x + first * core + second * (1 - core)) % 4,
            (z + first * (1 - core) + second * core) % 4,
        )

    def chip(first, second):
        there_x, there_z = at(first, second)
        return device_at(there_x, y, there_z, core)

    def run_device(steps):
        there = (run + steps + runs) % runs
        return ((there % 2) * 4 + y, there // 2)

    def y_device(steps):
        return device_at(x, (y + steps) % 4, z, core)

    sister = device_at(x, y, z, 1 - core)
    greet(
        [y_device(s) for s in (1, 2, 3)]
        + [chip(s, 0) for s in (1, 3)]
        + [chip(0, s) for s in (1, 3)]
        + [sister]
        + [run_device(s) for s in (1, 2, 3, 4, -1, -2, -3, -4)]
    )

    def half_rows(half):
        return pl.ds(0, SHARD_CUT) if half == 0 else pl.ds(SHARD_CUT, shard_rows - SHARD_CUT)

    def w_place(first, second, rows):
        there_x, there_z = at(first, second)
        lanes = pl.multiple_of((there_x // 2) * shard_cols, 128)
        return w_all.at[there_z * 4 + (there_x % 2) * 2 + core, rows, pl.ds(lanes, shard_cols)]

    own_seg = pltpu.make_async_copy(seg_ref, window_ref.at[0, y], own_sem.at[0])
    own_seg.start()
    seg_sent = [
        send(seg_ref, window_ref.at[0, y], sems, n, y_device(s)) for n, s in enumerate((1, 2, 3))
    ]

    every_row = pl.ds(0, shard_rows)
    own_w = pltpu.make_async_copy(shard_ref, w_place(0, 0, every_row), own_sem.at[1])
    own_w.start()
    own_half = lambda half: shard_ref.at[half_rows(half)]
    along = Ring(
        own_half, lambda o, h: w_place(o, 0, half_rows(h)), lambda s: chip(s, 0), sems, 8
    )

    def across(owner, number):
        own = own_half if owner == 0 else (lambda h: w_place(owner, 0, half_rows(h)))
        return Ring(
            own,
            lambda o, h: w_place(owner, o, half_rows(h)),
            lambda s: chip(0, s),
            sems,
            14 + 6 * number,
        )

    to_sister = []

    def hand_over(first, second):
        place = w_place(first, second, every_row)
        source = shard_ref if (first, second) == (0, 0) else place
        to_sister.append(send(source, place, sems, 38 + len(to_sister), sister))

    rings = [across(0, 0)]
    hand_over(0, 0)

    raw = xt_ref[...].astype(jnp.float32).T
    mean_square = jnp.sum(raw * raw, axis=1, keepdims=True) * (1.0 / width)
    normed_ref[...] = (raw * lax.rsqrt(mean_square + eps_norm) * gain_ref[...]).astype(jnp.bfloat16)

    own_seg.wait()
    for copy in seg_sent:
        copy.wait_recv()
    seg_on = [
        send(window_ref.at[0], window_ref.at[s], sems, 2 + s, run_device(s)) for s in (1, 2, 3, 4)
    ]

    rows_x = normed_ref.shape[0] // 2
    x_place = lambda o, h: x_all.at[(y + o) % 4, pl.ds(h * rows_x, rows_x)]
    own_x = pltpu.make_async_copy(normed_ref, x_all.at[y], own_sem.at[2])
    own_x.start()
    tokens_ring = Ring(
        lambda h: normed_ref.at[pl.ds(h * rows_x, rows_x)], x_place, y_device, sems, 54
    )

    along.take_left()
    rings.append(across(3, 1))
    hand_over(3, 0)
    along.take_right()
    rings.append(across(1, 2))
    hand_over(1, 0)
    rings[0].take_left()
    rings[0].take_right()
    tokens_ring.take_left()
    tokens_ring.take_right()
    along.take_far()
    rings.append(across(2, 3))
    hand_over(2, 0)
    owners = (0, 3, 1, 2)
    for number, owner in enumerate(owners):
        if number:
            rings[number].take_left()
        hand_over(owner, 3)
        if number:
            rings[number].take_right()
        hand_over(owner, 1)
        if number == 0:
            for copy in seg_on:
                copy.wait_recv()
            fill_tables(run, window_ref, freq_ref, cos_ref, sin_ref, pos_ref)
    for number, owner in enumerate(owners):
        rings[number].take_far()
        hand_over(owner, 2)
    tokens_ring.take_far()
    own_w.wait()
    own_x.wait()
    for copy in to_sister:
        copy.wait()
    for ring in [along, tokens_ring] + rings:
        ring.close()
    for copy in seg_sent + seg_on:
        copy.wait_send()


def fill_tables(run, window_ref, freq_ref, cos_ref, sin_ref, pos_ref):
    span, parts, _, lanes = window_ref.shape
    ids = [
        jnp.where(run - s >= 0, window_ref[s].reshape(parts * 8, lanes), -1).astype(jnp.float32)
        for s in range(span)
    ]
    ids = jnp.concatenate(ids, axis=0)
    fewer = [
        jnp.sum((ids < float(s)).astype(jnp.float32), keepdims=True) * 0.125 for s in range(SEGS)
    ]
    lane = lax.broadcasted_iota(jnp.int32, (lanes, lanes), 1)
    row = lax.broadcasted_iota(jnp.int32, (lanes, lanes), 0).astype(jnp.float32)
    for part in range(parts):
        own = window_ref[0, part].astype(jnp.float32)
        own = jnp.broadcast_to(own[0:1, :], (lanes, lanes)).T
        start = jnp.zeros((lanes, lanes), jnp.float32)
        for s in range(SEGS):
            start = jnp.where(own == float(s), fewer[s], start)
        position = row + float((span - 1) * parts * lanes + part * lanes) - start
        angle = position * freq_ref[...]
        turns = jnp.floor(angle * (0.5 / math.pi) + 0.5)
        angle = (angle - turns * 6.28125) - turns * (2.0 * math.pi - 6.28125)
        sine = jnp.sin(angle)
        here = pl.ds(part * lanes, lanes)
        cos_ref[here, :] = jnp.cos(angle)
        sin_ref[here, :] = jnp.where(lane % HD < HD // 2, -sine, sine)
        pos_ref[here, :] = position


def turned(tile, cosine, sine):
    lane = lax.broadcasted_iota(jnp.int32, tile.shape, 1)
    other = jnp.where(
        lane % HD < HD // 2, pltpu.roll(tile, 128 - HD // 2, 1), pltpu.roll(tile, HD // 2, 1)
    )
    return tile * cosine + other * sine


def attention_kernel(
    x_all,
    w_all,
    cos_ref,
    sin_ref,
    pos_ref,
    parts,
    kv_out,
    x_ref,
    w_ref,
    query_ref,
    kv_ref,
    sum_ref,
    send_sem,
    recv_sem,
    own_sem,
):
    x, y, z, core = chip_place()
    half = x // 2
    sems = (send_sem, recv_sem)
    run = lax.axis_index("col") * 2 + half
    runs = 2 * lax.axis_size("col")
    blocks, rows, padded = x_ref.shape

    def run_device(steps):
        there = (run + steps + runs) % runs
        return ((there % 2) * 4 + y, there // 2)

    def y_device(steps):
        return device_at(x, (y + steps) % 4, z, core)

    loads = [pltpu.make_async_copy(x_all, x_ref, own_sem.at[0])]
    query_cols = query_ref.shape[1] // 2
    shard_cols = w_ref.shape[1] // 2
    for h in range(2):
        lanes = pl.ds(h * shard_cols, query_cols + 2 * HD)
        loads.append(
            pltpu.make_async_copy(w_all.at[:, lanes], w_ref.at[:, lanes], own_sem.at[1 + h])
        )
    for h in range(2):
        lanes = pl.ds(h * shard_cols + query_cols + 2 * HD, query_cols)
        loads.append(
            pltpu.make_async_copy(w_all.at[:, lanes], w_ref.at[:, lanes], own_sem.at[3 + h])
        )
    for load in loads:
        load.start()
    partner = device_at((x + 2) % 4, y, z, core)
    greet([y_device(s) for s in (1, 2, 3)] + [run_device(1), run_device(-1), partner])

    loads[0].wait()
    cosine, sine = cos_ref[...], sin_ref[...]
    lane = lax.broadcasted_iota(jnp.int32, cosine.shape, 1)
    every = blocks * rows
    source = x_ref[...].reshape(every, padded)
    for h in range(2):
        loads[1 + h].wait()
        first = h * shard_cols
        mixed_kv = jnp.dot(
            source,
            w_ref[:, first : first + query_cols + 2 * HD],
            preferred_element_type=jnp.float32,
        )
        kv = mixed_kv[:, query_cols:]
        kv = jnp.where(lane < HD, turned(kv, cosine, sine), kv)
        kv_ref[h, pl.ds(rows, every), :] = kv.astype(jnp.bfloat16)
        for k in range(query_cols // 128):
            tile = turned(mixed_kv[:, k * 128 : k * 128 + 128], cosine, sine)
            query_ref[:, h * query_cols + k * 128 : h * query_cols + k * 128 + 128] = (
                tile * HD**-0.5
            ).astype(jnp.bfloat16)
    edge = send(
        kv_ref.at[:, pl.ds(every, rows)], kv_ref.at[:, pl.ds(0, rows)], sems, 0, run_device(1)
    )
    mine = pl.ds(pl.multiple_of(half * every, every), every)
    cache_there = send(
        kv_ref.at[1 - half, pl.ds(rows, every)], kv_out.at[mine], sems, 1, partner
    )
    cache_here = pltpu.make_async_copy(
        kv_ref.at[half, pl.ds(rows, every)], kv_out.at[mine], own_sem.at[5]
    )
    cache_here.start()
    loads[3].wait()
    loads[4].wait()
    edge.wait_recv()
    heads = query_cols // HD
    distance = (
        rows
        + lax.broadcasted_iota(jnp.int32, (rows, 2 * rows), 0)
        - lax.broadcasted_iota(jnp.int32, (rows, 2 * rows), 1)
    ).astype(jnp.float32)

    def out_copy(step, block):
        return pltpu.make_async_remote_copy(
            src_ref=sum_ref.at[step],
            dst_ref=parts.at[y],
            send_sem=send_sem.at[2 + step],
            recv_sem=recv_sem.at[2 + step],
            device_id=device_at(x, block, z, core),
            device_id_type=pl.DeviceIdType.MESH,
        )

    def one_block(step, carry):
        block = (y + 3 - step) % 4
        here = pl.ds(pl.multiple_of(block * rows, rows), rows)
        position = pos_ref[here, :]
        position = jnp.concatenate([position, position], axis=1)
        allowed = (distance >= 0) & (distance < WIN) & (distance <= position)
        allowed = jnp.concatenate([allowed.astype(jnp.float32)] * heads, axis=0) > 0.5
        total = None
        for h in range(2):
            first = h * shard_cols
            keys = kv_ref[h, pl.ds(pl.multiple_of(block * rows, rows), 2 * rows), :]
            values = jnp.where(
                lax.broadcasted_iota(jnp.int32, keys.shape, 1) < HD,
                pltpu.roll(keys.astype(jnp.float32), HD, 1),
                1.0,
            ).astype(jnp.bfloat16)
            query = query_ref[here, h * query_cols : (h + 1) * query_cols]
            query = jnp.concatenate(
                [query[:, n * HD : (n + 1) * HD] for n in range(heads)], axis=0
            )
            scores = lax.dot_general(
                query,
                keys[:, :HD],
                (((1,), (1,)), ((), ())),
                preferred_element_type=jnp.float32,
            )
            scores = jnp.where(allowed, scores, masked_score)
            sink_rows = w_ref[176:184, first : first + 128].astype(jnp.float32)
            sink_row = jnp.sum(sink_rows[4:8], axis=0, keepdims=True)
            sink = jnp.concatenate(
                [jnp.broadcast_to(sink_row[:, n : n + 1], (rows, 1)) for n in range(heads)], axis=0
            )
            ceiling = jnp.maximum(jnp.max(scores, axis=1, keepdims=True), sink)
            expo = jnp.exp(scores - ceiling).astype(jnp.bfloat16)
            mass = jnp.dot(expo, values, preferred_element_type=jnp.float32)
            seen = mass[:, :HD] / (mass[:, HD : HD + 1] + jnp.exp(sink - ceiling))
            seen = jnp.concatenate(
                [seen[n * rows : (n + 1) * rows] for n in range(heads)], axis=1
            ).astype(jnp.bfloat16)
            part = lax.dot_general(
                seen,
                w_ref[:, first + query_cols + 2 * HD : first + shard_cols],
                (((1,), (1,)), ((), ())),
                preferred_element_type=jnp.float32,
            )
            total = part if total is None else total + part
        sum_ref[step] = total.astype(jnp.bfloat16)

        @pl.when(step < blocks - 1)
        def _():
            out_copy(step, block).start()

        return carry

    lax.fori_loop(0, blocks, one_block, 0)
    own = pltpu.make_async_copy(sum_ref.at[blocks - 1], parts.at[y], own_sem.at[6])
    own.start()
    for step in range(blocks - 1):
        out_copy(step, (y + 3 - step) % 4).wait()
    own.wait()
    edge.wait_send()
    cache_there.wait()
    cache_here.wait()


def attention_layer(tokens, seg_ids, norm_gain, query_weight, kv_weight, out_weight, sinks):
    rows, width = tokens.shape
    col_count = lax.axis_size("col")
    share = query_weight.shape[0]
    padded_share = -(-share // 8) * 8
    extra = padded_share - share
    padded = padded_share * col_count
    xt = jnp.pad(tokens.T.reshape(col_count, share, rows), ((0, 0), (0, extra), (0, 0)))
    xt = xt.reshape(padded, rows)
    gain = jnp.pad(norm_gain.reshape(col_count, share), ((0, 0), (0, extra))).reshape(1, padded)
    shard = jnp.concatenate([query_weight, kv_weight, out_weight.T], axis=1)
    rest, sink_terms = sinks, []
    for _ in range(3):
        term = lax.reduce_precision(rest, 8, 7)
        sink_terms.append(term.astype(jnp.bfloat16))
        rest = rest - term
    sink_terms = jnp.pad(
        jnp.stack(sink_terms), ((0, extra - 3), (0, shard.shape[1] - sinks.shape[0]))
    )
    shard = jnp.concatenate([shard, sink_terms], axis=0)
    seg = jnp.broadcast_to(seg_ids[None, :], (8, rows))
    frequency = jnp.exp(
        (jnp.arange(128, dtype=jnp.int32) % (HD // 2)).astype(jnp.float32)
        * (-2.0 * math.log(theta_base) / HD)
    ).reshape(1, 128)
    vmem = pl.BlockSpec(memory_space=pltpu.VMEM)
    hbm = pl.BlockSpec(memory_space=pl.ANY)
    bf16, f32 = jnp.bfloat16, jnp.float32
    run_rows = 4 * rows
    table = jax.ShapeDtypeStruct((run_rows, 128), f32)
    shard_cols = shard.shape[1]
    x_all, w_all, cosine, sine, position = pl.pallas_call(
        functools.partial(gather_kernel, width),
        out_shape=(
            jax.ShapeDtypeStruct((4, rows, padded), bf16),
            jax.ShapeDtypeStruct((col_count, padded_share, 2 * shard_cols), bf16),
            table,
            table,
            table,
        ),
        in_specs=[vmem, vmem, hbm, vmem, hbm],
        out_specs=(hbm, hbm, vmem, vmem, vmem),
        scratch_shapes=[
            pltpu.VMEM((rows, padded), bf16),
            pltpu.VMEM((5, 4, 8, rows), jnp.int32),
            pltpu.SemaphoreType.DMA((60,)),
            pltpu.SemaphoreType.DMA((60,)),
            pltpu.SemaphoreType.DMA((3,)),
        ],
        compiler_params=pltpu.CompilerParams(
            collective_id=3, has_side_effects=True, vmem_limit_bytes=40 * 2**20
        ),
        name="gather_front",
    )(xt, gain, seg, frequency, shard)
    parts, kv_cache = pl.pallas_call(
        attention_kernel,
        out_shape=(
            jax.ShapeDtypeStruct((4, rows, padded), bf16),
            jax.ShapeDtypeStruct((2 * run_rows, 2 * HD), bf16),
        ),
        in_specs=[hbm, hbm, vmem, vmem, vmem],
        out_specs=(hbm, hbm),
        scratch_shapes=[
            pltpu.VMEM((4, rows, padded), bf16),
            pltpu.VMEM((padded, 2 * shard_cols), bf16),
            pltpu.VMEM((run_rows, 16 * HD), bf16),
            pltpu.VMEM((2, 5 * rows, 2 * HD), bf16),
            pltpu.VMEM((4, rows, padded), bf16),
            pltpu.SemaphoreType.DMA((6,)),
            pltpu.SemaphoreType.DMA((6,)),
            pltpu.SemaphoreType.DMA((7,)),
        ],
        compiler_params=pltpu.CompilerParams(
            collective_id=4, has_side_effects=True, vmem_limit_bytes=58 * 2**20
        ),
        name="attention",
    )(x_all, w_all.reshape(padded, 2 * shard_cols), cosine, sine, position)
    return parts, kv_cache, xt


def slot_grid(routes_t, tokens_here):
    expert_ids = lax.broadcasted_iota(jnp.int32, (EXPERTS, tokens_here), 0)
    hit = jnp.zeros((EXPERTS, tokens_here), jnp.float32)
    for j in range(TOP):
        hit = hit + (routes_t[j : j + 1, :] == expert_ids).astype(jnp.float32)
    earlier = (
        lax.broadcasted_iota(jnp.int32, (tokens_here, tokens_here), 0)
        < lax.broadcasted_iota(jnp.int32, (tokens_here, tokens_here), 1)
    ).astype(jnp.bfloat16)
    rank = jnp.dot(hit.astype(jnp.bfloat16), earlier, preferred_element_type=jnp.float32)
    return hit, rank


def by_slot(hit, rank, amount):
    tokens_here = hit.shape[1]
    slot_ids = lax.broadcasted_iota(jnp.int32, (EXPERTS, 8, tokens_here), 1).astype(jnp.float32)
    first = jnp.where(
        (hit[:, None, :] > 0.5) & (rank[:, None, :] == slot_ids), amount[:, None, :], 0.0
    ).reshape(EXPERTS * 8, tokens_here)
    last = jnp.where((hit > 0.5) & (rank == 8.0), amount, 0.0)
    return first, last


def tiles_of(width):
    return [(k, k * 128, min(128, width - k * 128)) for k in range(-(-width // 128))]


def widen(tile):
    short = 128 - tile.shape[1]
    if short:
        tile = jnp.concatenate([tile, jnp.zeros((tile.shape[0], short), tile.dtype)], axis=1)
    return tile


def pack_message(out_ref, last_ref, tile_first, tile_last, k):
    out_ref[:, k] = widen(tile_first).reshape(EXPERTS, 8, 128).astype(jnp.bfloat16)
    last_ref[pl.ds(k, EXPERTS, stride=24), :] = widen(tile_last)


def finish_message(out_ref, last_ref, tile_count):
    for k in range(tile_count, 24):
        last_ref[pl.ds(k, EXPERTS, stride=24), :] = jnp.zeros((EXPERTS, 128), jnp.float32)
    out_ref[:, tile_count:] = (
        last_ref[...].reshape(EXPERTS, 3, 8, 128).astype(jnp.bfloat16)
    )


def unpack_last(in_ref, last_ref, tile_count):
    last_ref[...] = in_ref[:, tile_count:].astype(jnp.float32).reshape(EXPERTS * 24, 128)


def unpack_tile(in_ref, last_ref, k):
    first = in_ref[:, k].astype(jnp.float32).reshape(EXPERTS * 8, 128)
    last = last_ref[pl.ds(k, EXPERTS, stride=24), :]
    return jnp.concatenate([first, last], axis=0).astype(jnp.bfloat16)


def dispatch_kernel(share, xt_ref, parts_ref, gain_ref, routes_ref, out_ref, hidden_ref, last_ref):
    total = xt_ref[...].astype(jnp.float32).T
    for part in range(parts_ref.shape[0]):
        total = total + parts_ref[part].astype(jnp.float32)
    padded_share = -(-share // 8) * 8
    hidden = jnp.concatenate(
        [total[:, i : i + share] for i in range(0, total.shape[1], padded_share)], axis=1
    )
    hidden_ref[...] = hidden
    moe_in = rms_scale(hidden, gain_ref[...], hidden.shape[1]).astype(jnp.bfloat16)
    hit, rank = slot_grid(routes_ref[...], hidden.shape[0])
    first, last = by_slot(hit, rank, jnp.ones_like(hit))
    first, last = first.astype(jnp.bfloat16), last.astype(jnp.bfloat16)
    tiles = tiles_of(hidden.shape[1])
    for k, start, width in tiles:
        piece = moe_in[:, start : start + width]
        pack_message(
            out_ref,
            last_ref,
            jnp.dot(first, piece, preferred_element_type=jnp.float32),
            jnp.dot(last, piece, preferred_element_type=jnp.float32),
            k,
        )
    finish_message(out_ref, last_ref, len(tiles))


def combine_kernel(hidden_ref, routes_ref, weights_ref, in_ref, out_ref, last_ref):
    routes_t, weights_t = routes_ref[...], weights_ref[...]
    tokens_here = routes_t.shape[1]
    hit, rank = slot_grid(routes_t, tokens_here)
    expert_ids = lax.broadcasted_iota(jnp.int32, (EXPERTS, tokens_here), 0)
    amount = jnp.zeros((EXPERTS, tokens_here), jnp.float32)
    for j in range(TOP):
        amount = amount + jnp.where(
            routes_t[j : j + 1, :] == expert_ids, weights_t[j : j + 1, :], 0.0
        )
    mix = jnp.concatenate(by_slot(hit, rank, amount), axis=0).T
    mix_high = mix.astype(jnp.bfloat16)
    mix_low = (mix - mix_high.astype(jnp.float32)).astype(jnp.bfloat16)
    tiles = tiles_of(out_ref.shape[0])
    unpack_last(in_ref, last_ref, len(tiles))
    for k, start, width in tiles:
        rows = unpack_tile(in_ref, last_ref, k)
        total = jnp.dot(mix_high, rows, preferred_element_type=jnp.float32) + jnp.dot(
            mix_low, rows, preferred_element_type=jnp.float32
        )
        here = slice(start, start + width)
        total = (widen(hidden_ref[:, here]) + total).T
        out_ref[here, :] = total[:width].astype(jnp.bfloat16)


def expert_kernel(
    in_ref, gate_a, up_a, down_a, gate_b, up_b, down_b, out_ref, rows_ref, total_ref, last_ref
):
    half, step = pl.program_id(0), pl.program_id(1)
    width = total_ref.shape[1]
    tiles = tiles_of(width)

    @pl.when((half == 0) & (step == 0))
    def _():
        unpack_last(in_ref, last_ref, len(tiles))
        for k, start, wide in tiles:
            rows_ref[:, start : start + wide] = unpack_tile(in_ref, last_ref, k)[:, :wide]

    def run(gate, up, down, fresh):
        rows = rows_ref[...]
        gate_part = jnp.dot(rows, gate[0], preferred_element_type=jnp.float32)
        up_part = jnp.dot(rows, up[0], preferred_element_type=jnp.float32)
        act = (gate_part * jax.nn.sigmoid(glu_alpha * gate_part) * (up_part + 1.0)).astype(
            jnp.bfloat16
        )
        part = lax.dot_general(
            act, down[0], (((1,), (1,)), ((), ())), preferred_element_type=jnp.float32
        )
        if fresh:
            total_ref[...] = part
        else:
            total_ref[...] += part

    @pl.when((half == 0) & (step == 0))
    def _():
        run(gate_a, up_a, down_a, True)

    @pl.when((half == 0) & (step != 0))
    def _():
        run(gate_a, up_a, down_a, False)

    @pl.when(half == 1)
    def _():
        run(gate_b, up_b, down_b, False)

    @pl.when((half == 1) & (step == pl.num_programs(1) - 1))
    def _():
        for k, start, wide in tiles:
            tile = total_ref[:, start : start + wide]
            pack_message(out_ref, last_ref, tile[: EXPERTS * 8], tile[EXPERTS * 8 :], k)
        finish_message(out_ref, last_ref, len(tiles))


def run_experts(arrived, own_in, own_out, peer_in, peer_out):
    width, half_width = own_in.shape[1], own_out.shape[2]
    chunk = 256
    steps = half_width // chunk
    first = lambda h, s: jnp.where(h == 0, s, steps - 1)
    second = lambda h, s: jnp.where(h == 0, 0, s)
    block_in, block_out = (1, width, chunk), (1, width, chunk)
    specs = []
    for pick in (first, second):
        specs += [
            pl.BlockSpec(block_in, lambda h, s, pick=pick: (0, 0, pick(h, s))),
            pl.BlockSpec(block_in, lambda h, s, pick=pick: (0, 0, pick(h, s) + steps)),
            pl.BlockSpec(block_out, lambda h, s, pick=pick: (0, 0, pick(h, s))),
        ]
    rows = EXPERTS * CAP
    return pl.pallas_call(
        expert_kernel,
        grid=(2, steps),
        out_shape=jax.ShapeDtypeStruct(arrived.shape, arrived.dtype),
        in_specs=[pl.BlockSpec(memory_space=pltpu.VMEM)] + specs,
        out_specs=pl.BlockSpec(memory_space=pltpu.VMEM),
        scratch_shapes=[
            pltpu.VMEM((rows, width), jnp.bfloat16),
            pltpu.VMEM((rows, width), jnp.float32),
            pltpu.VMEM((EXPERTS * 24, 128), jnp.float32),
        ],
        compiler_params=pltpu.CompilerParams(vmem_limit_bytes=60 * 2**20),
        name="experts",
    )(arrived, own_in, own_in, own_out, peer_in, peer_in, peer_out)


def expert_layer(share, xt, parts, moe_gain, routes, route_weights, own, peer):
    tokens_here = routes.shape[0]
    width = moe_gain.shape[0]
    vmem = pl.BlockSpec(memory_space=pltpu.VMEM)
    message = jax.ShapeDtypeStruct((EXPERTS, -(-width // 128) + 3, 8, 128), jnp.bfloat16)
    last = pltpu.VMEM((EXPERTS * 24, 128), jnp.float32)
    outgoing, hidden = pl.pallas_call(
        functools.partial(dispatch_kernel, share),
        out_shape=(message, jax.ShapeDtypeStruct((tokens_here, width), jnp.float32)),
        in_specs=[vmem] * 4,
        out_specs=(vmem, vmem),
        scratch_shapes=[last],
        compiler_params=pltpu.CompilerParams(vmem_limit_bytes=40 * 2**20),
        name="dispatch",
    )(xt, parts, moe_gain.reshape(1, width), routes.T)
    arrived = exchange(outgoing, 1, "exchange_out")
    produced = run_experts(arrived, *own, *peer)
    returned = exchange(produced, 2, "exchange_back")
    mixed = pl.pallas_call(
        combine_kernel,
        out_shape=jax.ShapeDtypeStruct((width, tokens_here), jnp.bfloat16),
        in_specs=[vmem] * 4,
        out_specs=vmem,
        scratch_shapes=[last],
        compiler_params=pltpu.CompilerParams(vmem_limit_bytes=40 * 2**20),
        name="combine",
    )(hidden, routes.T, route_weights.T, returned)
    return mixed.T


def shards(
    tokens,
    seg_ids,
    norm_gain,
    query_weight,
    kv_weight,
    out_weight,
    sinks,
    moe_gain,
    routes,
    route_weights,
    expert_in,
    expert_out,
):
    swap = [(c, c + 1 - 2 * (c % 2)) for c in range(lax.axis_size("col"))]
    own_in, own_out = expert_in, jnp.swapaxes(expert_out, 1, 2)
    peer_in, peer_out = (lax.ppermute(w, "col", swap) for w in (own_in, own_out))
    parts, kv_cache, xt = attention_layer(
        tokens, seg_ids, norm_gain, query_weight, kv_weight, out_weight, sinks
    )
    mixed = expert_layer(
        query_weight.shape[0],
        xt,
        parts,
        moe_gain,
        routes,
        route_weights,
        (own_in, own_out),
        (peer_in, peer_out),
    )
    return (mixed, kv_cache)


def solution(mesh):
    in_specs = (
        P(("col", "row"), None),
        P(("col", "row")),
        P(),
        P("col", "row"),
        P("col", "row"),
        P("row", "col"),
        P("row"),
        P(),
        P(("col", "row"), None),
        P(("col", "row"), None),
        P(("row", "col"), None, None),
        P(("row", "col"), None, None),
    )
    out_specs = (P(("col", "row"), None), P("col", "row"))
    return jax.shard_map(shards, mesh=mesh, in_specs=in_specs, out_specs=out_specs, check_vma=False)
```

```python
import functools
import math

import jax
import jax.numpy as jnp
import numpy as np
from jax import lax
from jax.experimental import pallas as pl
from jax.experimental.pallas import tpu as pltpu
from jax.sharding import PartitionSpec as P

HD = 64
WIN = 128
EXPERTS = 64
TOP = 4
CAP = 9
SEGS = 16


eps_norm = 1e-05
theta_base = 150000.0
glu_alpha = 1.702
masked_score = -1e30


def rms_scale(widened, gain_vec, width):
    mean_square = jnp.sum(widened * widened, axis=-1, keepdims=True) * (1.0 / width)
    return widened * lax.rsqrt(mean_square + eps_norm) * gain_vec


def chip_place():
    row, col = lax.axis_index("row"), lax.axis_index("col")
    return (row // 4) * 2 + (col // 2) % 2, row % 4, col // 4, col % 2


def device_at(x, y, z, core):
    return ((x // 2) * 4 + y, z * 4 + (x % 2) * 2 + core)


def expert_at(x, y, z):
    return ((x // 2) * 4 + y) * 8 + z * 2 + x % 2


def hop_order():
    every = [
        (dx, (t + dx) % 4, (t // 4 + dx) % 4) for t in range(16) for dx in (1, 3, 2, 0)
    ]
    return [v for v in every if v != (0, 0, 0)]


def exchange_kernel(out_msgs, in_msgs, send_sem, recv_sem, own_sem):
    x, y, z, core = chip_place()
    me = expert_at(x, y, z)
    offsets = hop_order()
    barrier = pltpu.get_barrier_semaphore()
    for dx, dy, dz in offsets:
        pl.semaphore_signal(
            barrier,
            inc=1,
            device_id=device_at((x + dx) % 4, (y + dy) % 4, (z + dz) % 4, core),
            device_id_type=pl.DeviceIdType.MESH,
        )
    own = pltpu.make_async_copy(out_msgs.at[me], in_msgs.at[me], own_sem)
    own.start()
    pl.semaphore_wait(barrier, len(offsets))
    copies = []
    for number, (dx, dy, dz) in enumerate(offsets):
        there = ((x + dx) % 4, (y + dy) % 4, (z + dz) % 4)
        copy = pltpu.make_async_remote_copy(
            src_ref=out_msgs.at[expert_at(*there)],
            dst_ref=in_msgs.at[me],
            send_sem=send_sem.at[number],
            recv_sem=recv_sem.at[number],
            device_id=device_at(*there, core),
            device_id_type=pl.DeviceIdType.MESH,
        )
        copy.start()
        copies.append(copy)
    own.wait()
    for copy in copies:
        copy.wait()


def exchange(messages, ident, name):
    others = EXPERTS - 1
    return pl.pallas_call(
        exchange_kernel,
        out_shape=jax.ShapeDtypeStruct(messages.shape, messages.dtype),
        in_specs=[pl.BlockSpec(memory_space=pl.ANY)],
        out_specs=pl.BlockSpec(memory_space=pl.ANY),
        scratch_shapes=[
            pltpu.SemaphoreType.DMA((others,)),
            pltpu.SemaphoreType.DMA((others,)),
            pltpu.SemaphoreType.DMA,
        ],
        compiler_params=pltpu.CompilerParams(collective_id=ident, has_side_effects=True),
        name=name,
    )(messages)


def described(source, target, sems, number, device):
    return pltpu.make_async_remote_copy(
        src_ref=source,
        dst_ref=target,
        send_sem=sems[0].at[number],
        recv_sem=sems[1].at[number],
        device_id=device,
        device_id_type=pl.DeviceIdType.MESH,
    )


def send(*parts):
    copy = described(*parts)
    copy.start()
    return copy


def greet(devices):
    barrier = pltpu.get_barrier_semaphore()
    for device in devices:
        pl.semaphore_signal(
            barrier, inc=1, device_id=device, device_id_type=pl.DeviceIdType.MESH
        )
    pl.semaphore_wait(barrier, len(devices))


class Ring:
    def __init__(self, own, place, device, sems, first):
        self.place, self.device, self.sems, self.first = place, device, sems, first
        self.sent = [
            self.pass_on(0, own(0), 0, 0, 1),
            self.pass_on(1, own(1), 0, 1, 1),
            self.pass_on(2, own(1), 0, 1, 3),
            self.pass_on(3, own(0), 0, 0, 3),
        ]

    def pass_on(self, number, source, owner, half, to):
        return send(
            source, self.place(owner, half), self.sems, self.first + number, self.device(to)
        )

    def take_left(self):
        self.sent[0].wait_recv()
        self.sent.append(self.pass_on(4, self.place(3, 0), 3, 0, 1))
        self.sent[1].wait_recv()

    def take_right(self):
        self.sent[2].wait_recv()
        self.sent.append(self.pass_on(5, self.place(1, 1), 1, 1, 3))
        self.sent[3].wait_recv()

    def take_far(self):
        self.sent[4].wait_recv()
        self.sent[5].wait_recv()

    def close(self):
        for copy in self.sent:
            copy.wait_send()


SHARD_CUT = 96
QUERY_LANES = 8 * HD
PROJ_LANES = QUERY_LANES + 2 * HD


def front_kernel(
    width,
    share,
    xt_ref,
    gain_ref,
    seg_ref,
    freq_ref,
    shard_ref,
    routes_ref,
    out_ref,
    hidden_ref,
    kv_out,
    x_ref,
    w_ref,
    window_ref,
    cos_ref,
    sin_ref,
    pos_ref,
    query_ref,
    kv_ref,
    sum_ref,
    far_ref,
    parts_ref,
    last_ref,
    send_sem,
    recv_sem,
    own_sem,
):
    x, y, z, core = chip_place()
    sems = (send_sem, recv_sem)
    side = x // 2
    run = lax.axis_index("col") * 2 + side
    runs = 2 * lax.axis_size("col")
    shard_rows = shard_ref.shape[0]
    blocks, rows, padded = x_ref.shape
    every = blocks * rows

    def at(first, second):
        return (
            (x + first * core + second * (1 - core)) % 4,
            (z + first * (1 - core) + second * core) % 4,
        )

    def chip(first, second):
        there_x, there_z = at(first, second)
        return device_at(there_x, y, there_z, core)

    def run_device(steps):
        there = (run + steps + runs) % runs
        return ((there % 2) * 4 + y, there // 2)

    def y_device(steps):
        return device_at(x, (y + steps) % 4, z, core)

    sister = device_at(x, y, z, 1 - core)
    partner = device_at((x + 2) % 4, y, z, core)
    greet(
        [y_device(s) for s in (1, 2, 3)]
        + [chip(s, 0) for s in (1, 3)]
        + [chip(0, s) for s in (1, 3)]
        + [sister, partner]
        + [run_device(s) for s in (1, 2, 3, 4, -1, -2, -3, -4)]
    )
    own_seg = pltpu.make_async_copy(seg_ref, window_ref.at[0, y], own_sem.at[0])
    own_seg.start()
    seg_sent = [
        send(seg_ref, window_ref.at[0, y], sems, n, y_device(s)) for n, s in enumerate((1, 2, 3))
    ]

    class Stream:
        def __init__(self, first_sem):
            self.first_sem = first_sem
            self.to_sister, self.rings = [], {}
            self.own = pltpu.make_async_copy(
                self.shard(pl.ds(0, shard_rows)),
                self.place(0, 0, pl.ds(0, shard_rows)),
                own_sem.at[1],
            )
            self.own.start()
            self.along = Ring(
                self.own_half,
                lambda o, h: self.half(o, 0, h),
                lambda s: chip(s, 0),
                sems,
                first_sem,
            )
            self.across(0)

        def shard(self, rows_here):
            return shard_ref.at[rows_here]

        def place(self, first, second, rows_here):
            there_x, there_z = at(first, second)
            slot = there_z * 4 + (there_x % 2) * 2 + core
            start = pl.multiple_of(slot * shard_rows + rows_here.start, 16)
            return w_ref.at[there_x // 2, pl.ds(start, rows_here.size)]

        def cut(self, half):
            if half == 0:
                return pl.ds(0, SHARD_CUT)
            return pl.ds(SHARD_CUT, shard_rows - SHARD_CUT)

        def own_half(self, half):
            return self.shard(self.cut(half))

        def half(self, first, second, half):
            return self.place(first, second, self.cut(half))

        def across(self, owner):
            own = self.own_half if owner == 0 else (lambda h: self.half(owner, 0, h))
            self.rings[owner] = Ring(
                own,
                lambda o, h: self.half(owner, o, h),
                lambda s: chip(0, s),
                sems,
                self.first_sem + 6 + 6 * len(self.rings),
            )
            self.hand_over(owner, 0)

        def hand_over(self, first, second):
            place = self.place(first, second, pl.ds(0, shard_rows))
            own = (first, second) == (0, 0)
            source = self.shard(pl.ds(0, shard_rows)) if own else place
            number = self.first_sem + 30 + len(self.to_sister)
            self.to_sister.append(send(source, place, sems, number, sister))

        def near(self, owner):
            self.rings[owner].take_left()
            self.hand_over(owner, 3)
            self.rings[owner].take_right()
            self.hand_over(owner, 1)

        def far(self, owner):
            self.rings[owner].take_far()
            self.hand_over(owner, 2)

        def arrived(self):
            self.own.wait()
            for copy in self.to_sister:
                copy.wait_recv()

        def close(self):
            for ring in [self.along] + list(self.rings.values()):
                ring.close()
            for copy in self.to_sister:
                copy.wait_send()

    proj = Stream(20)

    raw = xt_ref[...].astype(jnp.float32).T
    normed = rms_scale(raw, gain_ref[0:1, :], width)
    gap = jnp.zeros((rows, shard_rows - share), jnp.float32)
    x_ref[y] = jnp.concatenate(
        [piece for i in range(0, width, share) for piece in (normed[:, i : i + share], gap)],
        axis=1,
    ).astype(jnp.bfloat16)

    own_seg.wait()
    for copy in seg_sent:
        copy.wait_recv()
    seg_on = [
        send(window_ref.at[0], window_ref.at[s], sems, 2 + s, run_device(s)) for s in (1, 2, 3, 4)
    ]
    half_rows = rows // 2
    upper, lower = pl.ds(0, half_rows), pl.ds(half_rows, half_rows)
    x_place = lambda o, h: x_ref.at[(y + o) % 4, lower if h else upper]
    tokens_ring = Ring(lambda h: x_place(0, h), x_place, y_device, sems, 7)

    proj.along.take_left()
    proj.across(3)
    proj.along.take_right()
    proj.across(1)
    proj.rings[0].take_left()
    proj.hand_over(0, 3)
    proj.rings[0].take_right()
    proj.hand_over(0, 1)
    tokens_ring.take_left()
    tokens_ring.take_right()
    proj.along.take_far()
    proj.across(2)
    proj.near(3)
    for copy in seg_on:
        copy.wait_recv()
    fill_tables(run, window_ref, freq_ref, cos_ref, sin_ref, pos_ref)
    proj.near(1)
    proj.near(2)
    for owner in (0, 3, 1, 2):
        proj.far(owner)
    tokens_ring.take_far()
    proj.arrived()

    cosine, sine = cos_ref[...], sin_ref[...]
    lane = lax.broadcasted_iota(jnp.int32, cosine.shape, 1)

    edges = []

    def project(h):
        mixed_kv = jnp.dot(
            x_ref[...].reshape(every, padded),
            w_ref[h, :, :PROJ_LANES],
            preferred_element_type=jnp.float32,
        )
        kv = mixed_kv[:, QUERY_LANES:]
        kv = jnp.where(lane < HD, turned(kv, cosine, sine), kv)
        kv_ref[h, pl.ds(rows, every), :] = kv.astype(jnp.bfloat16)
        edges.append(
            send(
                kv_ref.at[h, pl.ds(every, rows)],
                kv_ref.at[h, pl.ds(0, rows)],
                sems,
                66 + h,
                run_device(1),
            )
        )
        for k in range(0, QUERY_LANES, 128):
            tile = turned(mixed_kv[:, k : k + 128], cosine, sine) * HD**-0.5
            query_ref[:, h * QUERY_LANES + k : h * QUERY_LANES + k + 128] = tile.astype(
                jnp.bfloat16
            )

    project(0)
    project(1)
    mine = pl.ds(pl.multiple_of(side * every, every), every)
    cache_there = send(
        kv_ref.at[1 - side, pl.ds(rows, every)], kv_out.at[mine], sems, 14, partner
    )
    cache_here = pltpu.make_async_copy(
        kv_ref.at[side, pl.ds(rows, every)], kv_out.at[mine], own_sem.at[3]
    )
    cache_here.start()
    for edge in edges:
        edge.wait_recv()
    distance = (
        rows
        + lax.broadcasted_iota(jnp.int32, (rows, 2 * rows), 0)
        - lax.broadcasted_iota(jnp.int32, (rows, 2 * rows), 1)
    ).astype(jnp.float32)

    right, left = y_device(1), y_device(3)
    far_a = (sum_ref.at[0, upper], far_ref.at[0], sems, 15, right)
    far_b = (sum_ref.at[0, lower], far_ref.at[1], sems, 16, left)
    right_b = (sum_ref.at[1, lower], parts_ref.at[0, lower], sems, 17, right)
    left_a = (sum_ref.at[2, upper], parts_ref.at[1, upper], sems, 18, left)
    right_a = (sum_ref.at[1, upper], parts_ref.at[0, upper], sems, 19, right)
    left_b = (sum_ref.at[2, lower], parts_ref.at[1, lower], sems, 13, left)

    def one_block(step, carry):
        block = (y + 10 - step + (step // 2) * (7 - 2 * step)) % 4
        here = pl.ds(pl.multiple_of(block * rows, rows), rows)
        sum_ref[step] = block_sum(
            here,
            pl.ds(pl.multiple_of(block * rows, rows), 2 * rows),
            distance,
            pos_ref,
            query_ref,
            kv_ref,
            w_ref,
        ).astype(jnp.bfloat16)

        @pl.when(step == 0)
        def _():
            send(*far_a)
            send(*far_b)

        @pl.when(step == 1)
        def _():
            send(*right_b)

        @pl.when(step == 2)
        def _():
            send(*left_a)

        return carry

    lax.fori_loop(0, blocks, one_block, 0)
    far_a, far_b, right_b, left_a = (described(*c) for c in (far_a, far_b, right_b, left_a))
    far_a.wait_recv()
    sum_ref[1, upper] = (
        sum_ref[1, upper].astype(jnp.float32) + far_ref[0].astype(jnp.float32)
    ).astype(jnp.bfloat16)
    right_a = send(*right_a)
    far_b.wait_recv()
    sum_ref[2, lower] = (
        sum_ref[2, lower].astype(jnp.float32) + far_ref[1].astype(jnp.float32)
    ).astype(jnp.bfloat16)
    left_b = send(*left_b)
    proj.close()
    tokens_ring.close()
    for copy in seg_sent + seg_on + edges + [far_a, far_b]:
        copy.wait_send()
    total = sum_ref[blocks - 1].astype(jnp.float32)
    hit, rank = slot_grid(routes_ref[...], rows)
    first, last = by_slot(hit, rank, jnp.ones_like(hit))
    for copy in (right_b, left_a, right_a, left_b, cache_there, cache_here):
        copy.wait()
    total = total + parts_ref[0].astype(jnp.float32) + parts_ref[1].astype(jnp.float32)
    hidden = jnp.concatenate(
        [total[:, i : i + share] for i in range(0, padded, shard_rows)], axis=1
    )
    hidden = hidden + xt_ref[...].astype(jnp.float32).T
    hidden_ref[...] = hidden
    moe_in = rms_scale(hidden, gain_ref[1:2, :], width).astype(jnp.bfloat16)
    first, last = first.astype(jnp.bfloat16), last.astype(jnp.bfloat16)
    tiles = tiles_of(width)
    for k, start, wide in tiles:
        piece = moe_in[:, start : start + wide]
        pack_message(
            out_ref,
            last_ref,
            jnp.dot(first, piece, preferred_element_type=jnp.float32),
            jnp.dot(last, piece, preferred_element_type=jnp.float32),
            k,
        )
    finish_message(out_ref, last_ref, len(tiles))


def block_sum(here, near, distance, pos_ref, query_ref, kv_ref, w_ref):
    rows = distance.shape[0]
    heads = QUERY_LANES // HD
    position = pos_ref[here, :]
    position = jnp.concatenate([position, position], axis=1)
    allowed = (distance >= 0) & (distance < WIN) & (distance <= position)
    allowed = jnp.concatenate([allowed.astype(jnp.float32)] * heads, axis=0) > 0.5
    total = None
    for h in range(2):
        keys = kv_ref[h, near, :]
        values = jnp.where(
            lax.broadcasted_iota(jnp.int32, keys.shape, 1) < HD,
            pltpu.roll(keys.astype(jnp.float32), HD, 1),
            1.0,
        ).astype(jnp.bfloat16)
        query = query_ref[here, h * QUERY_LANES : (h + 1) * QUERY_LANES]
        query = jnp.concatenate([query[:, n * HD : (n + 1) * HD] for n in range(heads)], axis=0)
        scores = lax.dot_general(
            query,
            keys[:, :HD],
            (((1,), (1,)), ((), ())),
            preferred_element_type=jnp.float32,
        )
        scores = jnp.where(allowed, scores, masked_score)
        sink_rows = w_ref[h, 176:192, 0:128].astype(jnp.float32)
        sink_row = jnp.sum(sink_rows[4:8], axis=0, keepdims=True)
        sink = jnp.concatenate(
            [jnp.broadcast_to(sink_row[:, n : n + 1], (rows, 1)) for n in range(heads)], axis=0
        )
        ceiling = jnp.maximum(jnp.max(scores, axis=1, keepdims=True), sink)
        expo = jnp.exp(scores - ceiling).astype(jnp.bfloat16)
        mass = jnp.dot(expo, values, preferred_element_type=jnp.float32)
        seen = mass[:, :HD] / (mass[:, HD : HD + 1] + jnp.exp(sink - ceiling))
        seen = jnp.concatenate(
            [seen[n * rows : (n + 1) * rows] for n in range(heads)], axis=1
        ).astype(jnp.bfloat16)
        part = lax.dot_general(
            seen,
            w_ref[h, :, PROJ_LANES:],
            (((1,), (1,)), ((), ())),
            preferred_element_type=jnp.float32,
        )
        total = part if total is None else total + part
    return total


def circle(angle):
    quarter = jnp.floor(angle * (2.0 / math.pi) + 0.5)
    rest = angle - quarter * 1.5703125
    rest = rest - quarter * 4.837512969970703125e-4
    rest = rest - quarter * 7.54978995489188216e-8
    square = rest * rest
    low = rest + rest * square * (
        -1.6666654611e-1 + square * (8.3321608736e-3 - square * 1.9515295891e-4)
    )
    high = (1.0 - 0.5 * square) + square * square * (
        4.166664568298827e-2 + square * (-1.388731625493765e-3 + square * 2.443315711809948e-5)
    )
    turn = quarter.astype(jnp.int32) % 4
    odd = turn % 2 == 1
    sine, cosine = jnp.where(odd, high, low), jnp.where(odd, low, high)
    return (
        jnp.where((turn == 1) | (turn == 2), -cosine, cosine),
        jnp.where(turn >= 2, -sine, sine),
    )


def fill_tables(run, window_ref, freq_ref, cos_ref, sin_ref, pos_ref):
    span, parts, _, lanes = window_ref.shape
    ids = [
        jnp.where(run - s >= 0, window_ref[s].reshape(parts * 8, lanes), -1).astype(jnp.float32)
        for s in range(span)
    ]
    ids = jnp.concatenate(ids, axis=0)
    fewer = [
        jnp.sum((ids < float(s)).astype(jnp.float32), keepdims=True) * 0.125 for s in range(SEGS)
    ]
    lane = lax.broadcasted_iota(jnp.int32, (lanes, lanes), 1)
    row = lax.broadcasted_iota(jnp.int32, (lanes, lanes), 0).astype(jnp.float32)
    for part in range(parts):
        own = window_ref[0, part].astype(jnp.float32)
        own = jnp.broadcast_to(own[0:1, :], (lanes, lanes)).T
        start = jnp.zeros((lanes, lanes), jnp.float32)
        for s in range(SEGS):
            start = jnp.where(own == float(s), fewer[s], start)
        position = row + float((span - 1) * parts * lanes + part * lanes) - start
        angle = position * freq_ref[...]
        cosine, sine = circle(angle)
        here = pl.ds(part * lanes, lanes)
        cos_ref[here, :] = cosine
        sin_ref[here, :] = jnp.where(lane % HD < HD // 2, -sine, sine)
        pos_ref[here, :] = position


def turned(tile, cosine, sine):
    lane = lax.broadcasted_iota(jnp.int32, tile.shape, 1)
    other = jnp.where(
        lane % HD < HD // 2, pltpu.roll(tile, 128 - HD // 2, 1), pltpu.roll(tile, HD // 2, 1)
    )
    return tile * cosine + other * sine


def attention_layer(
    tokens, seg_ids, norm_gain, query_weight, kv_weight, out_weight, sinks, moe_gain, routes
):
    rows, width = tokens.shape
    col_count = lax.axis_size("col")
    share = query_weight.shape[0]
    padded_share = -(-share // 16) * 16
    extra = padded_share - share
    padded = padded_share * col_count
    gains = jnp.stack([norm_gain, moe_gain])
    shard = jnp.concatenate([query_weight, kv_weight, out_weight.T], axis=1)
    rest, sink_terms = sinks, []
    for _ in range(3):
        term = lax.reduce_precision(rest, 8, 7)
        sink_terms.append(term.astype(jnp.bfloat16))
        rest = rest - term
    sink_terms = jnp.pad(
        jnp.stack(sink_terms), ((0, extra - 3), (0, shard.shape[1] - sinks.shape[0]))
    )
    shard = jnp.concatenate([shard, sink_terms], axis=0)
    seg = jnp.broadcast_to(seg_ids[None, :], (8, rows))
    frequency = jnp.asarray(
        np.exp((np.arange(128) % (HD // 2)) * (-2.0 * math.log(theta_base) / HD))[None, :],
        jnp.float32,
    )
    vmem = pl.BlockSpec(memory_space=pltpu.VMEM)
    hbm = pl.BlockSpec(memory_space=pl.ANY)
    bf16, f32 = jnp.bfloat16, jnp.float32
    sem = pltpu.SemaphoreType.DMA
    return pl.pallas_call(
        functools.partial(front_kernel, width, share),
        out_shape=(
            jax.ShapeDtypeStruct((EXPERTS, -(-width // 128) + 3, 8, 128), bf16),
            jax.ShapeDtypeStruct((rows, width), f32),
            jax.ShapeDtypeStruct((8 * rows, 2 * HD), bf16),
        ),
        in_specs=[vmem, vmem, hbm, vmem, hbm, vmem],
        out_specs=(vmem, vmem, hbm),
        scratch_shapes=[
            pltpu.VMEM((4, rows, padded), bf16),
            pltpu.VMEM((2, padded, shard.shape[1]), bf16),
            pltpu.VMEM((5, 4, 8, rows), jnp.int32),
            pltpu.VMEM((4 * rows, 128), f32),
            pltpu.VMEM((4 * rows, 128), f32),
            pltpu.VMEM((4 * rows, 128), f32),
            pltpu.VMEM((4 * rows, 2 * QUERY_LANES), bf16),
            pltpu.VMEM((2, 5 * rows, 2 * HD), bf16),
            pltpu.VMEM((4, rows, padded), bf16),
            pltpu.VMEM((2, rows // 2, padded), bf16),
            pltpu.VMEM((2, rows, padded), bf16),
            pltpu.VMEM((EXPERTS * 24, 128), f32),
            sem((68,)),
            sem((68,)),
            sem((4,)),
        ],
        compiler_params=pltpu.CompilerParams(
            collective_id=3, has_side_effects=True, vmem_limit_bytes=58 * 2**20
        ),
        name="front",
    )(tokens.T, gains, seg, frequency, shard, routes.T)


def slot_grid(routes_t, tokens_here):
    expert_ids = lax.broadcasted_iota(jnp.int32, (EXPERTS, tokens_here), 0)
    hit = jnp.zeros((EXPERTS, tokens_here), jnp.float32)
    for j in range(TOP):
        hit = hit + (routes_t[j : j + 1, :] == expert_ids).astype(jnp.float32)
    earlier = (
        lax.broadcasted_iota(jnp.int32, (tokens_here, tokens_here), 0)
        < lax.broadcasted_iota(jnp.int32, (tokens_here, tokens_here), 1)
    ).astype(jnp.bfloat16)
    rank = jnp.dot(hit.astype(jnp.bfloat16), earlier, preferred_element_type=jnp.float32)
    return hit, rank


def by_slot(hit, rank, amount):
    tokens_here = hit.shape[1]
    slot_ids = lax.broadcasted_iota(jnp.int32, (EXPERTS, 8, tokens_here), 1).astype(jnp.float32)
    first = jnp.where(
        (hit[:, None, :] > 0.5) & (rank[:, None, :] == slot_ids), amount[:, None, :], 0.0
    ).reshape(EXPERTS * 8, tokens_here)
    last = jnp.where((hit > 0.5) & (rank == 8.0), amount, 0.0)
    return first, last


def tiles_of(width):
    return [(k, k * 128, min(128, width - k * 128)) for k in range(-(-width // 128))]


def widen(tile):
    short = 128 - tile.shape[1]
    if short:
        tile = jnp.concatenate([tile, jnp.zeros((tile.shape[0], short), tile.dtype)], axis=1)
    return tile


def pack_message(out_ref, last_ref, tile_first, tile_last, k):
    out_ref[:, k] = widen(tile_first).reshape(EXPERTS, 8, 128).astype(jnp.bfloat16)
    last_ref[pl.ds(k, EXPERTS, stride=24), :] = widen(tile_last)


def finish_message(out_ref, last_ref, tile_count):
    for k in range(tile_count, 24):
        last_ref[pl.ds(k, EXPERTS, stride=24), :] = jnp.zeros((EXPERTS, 128), jnp.float32)
    out_ref[:, tile_count:] = (
        last_ref[...].reshape(EXPERTS, 3, 8, 128).astype(jnp.bfloat16)
    )


def unpack_last(in_ref, last_ref, tile_count):
    last_ref[...] = in_ref[:, tile_count:].astype(jnp.float32).reshape(EXPERTS * 24, 128)


def unpack_tile(in_ref, last_ref, k):
    first = in_ref[:, k].astype(jnp.float32).reshape(EXPERTS * 8, 128)
    last = last_ref[pl.ds(k, EXPERTS, stride=24), :]
    return jnp.concatenate([first, last], axis=0).astype(jnp.bfloat16)


def combine_kernel(hidden_ref, routes_ref, weights_ref, in_ref, out_ref, last_ref):
    routes_t, weights_t = routes_ref[...], weights_ref[...]
    tokens_here = routes_t.shape[1]
    hit, rank = slot_grid(routes_t, tokens_here)
    expert_ids = lax.broadcasted_iota(jnp.int32, (EXPERTS, tokens_here), 0)
    amount = jnp.zeros((EXPERTS, tokens_here), jnp.float32)
    for j in range(TOP):
        amount = amount + jnp.where(
            routes_t[j : j + 1, :] == expert_ids, weights_t[j : j + 1, :], 0.0
        )
    mix = jnp.concatenate(by_slot(hit, rank, amount), axis=0).T
    mix_high = mix.astype(jnp.bfloat16)
    mix_low = (mix - mix_high.astype(jnp.float32)).astype(jnp.bfloat16)
    tiles = tiles_of(out_ref.shape[0])
    unpack_last(in_ref, last_ref, len(tiles))
    for k, start, width in tiles:
        rows = unpack_tile(in_ref, last_ref, k)
        total = jnp.dot(mix_high, rows, preferred_element_type=jnp.float32) + jnp.dot(
            mix_low, rows, preferred_element_type=jnp.float32
        )
        here = slice(start, start + width)
        total = (widen(hidden_ref[:, here]) + total).T
        out_ref[here, :] = total[:width].astype(jnp.bfloat16)


def expert_kernel(
    in_ref, gate_a, up_a, down_a, gate_b, up_b, down_b, out_ref, rows_ref, total_ref, last_ref
):
    half, step = pl.program_id(0), pl.program_id(1)
    width = total_ref.shape[1]
    tiles = tiles_of(width)

    @pl.when((half == 0) & (step == 0))
    def _():
        unpack_last(in_ref, last_ref, len(tiles))
        for k, start, wide in tiles:
            rows_ref[:, start : start + wide] = unpack_tile(in_ref, last_ref, k)[:, :wide]

    def run(gate, up, down, fresh):
        rows = rows_ref[...]
        gate_part = jnp.dot(rows, gate[0], preferred_element_type=jnp.float32)
        up_part = jnp.dot(rows, up[0], preferred_element_type=jnp.float32)
        act = (gate_part * jax.nn.sigmoid(glu_alpha * gate_part) * (up_part + 1.0)).astype(
            jnp.bfloat16
        )
        part = lax.dot_general(
            act, down[0], (((1,), (1,)), ((), ())), preferred_element_type=jnp.float32
        )
        if fresh:
            total_ref[...] = part
        else:
            total_ref[...] += part

    @pl.when((half == 0) & (step == 0))
    def _():
        run(gate_a, up_a, down_a, True)

    @pl.when((half == 0) & (step != 0))
    def _():
        run(gate_a, up_a, down_a, False)

    @pl.when(half == 1)
    def _():
        run(gate_b, up_b, down_b, False)

    @pl.when((half == 1) & (step == pl.num_programs(1) - 1))
    def _():
        for k, start, wide in tiles:
            tile = total_ref[:, start : start + wide]
            pack_message(out_ref, last_ref, tile[: EXPERTS * 8], tile[EXPERTS * 8 :], k)
        finish_message(out_ref, last_ref, len(tiles))


def run_experts(arrived, own_in, own_out, peer_in, peer_out):
    width, half_width = own_in.shape[1], own_out.shape[2]
    chunk = 256
    steps = half_width // chunk
    first = lambda h, s: jnp.where(h == 0, s, steps - 1)
    second = lambda h, s: jnp.where(h == 0, 0, s)
    block_in, block_out = (1, width, chunk), (1, width, chunk)
    specs = []
    for pick in (first, second):
        specs += [
            pl.BlockSpec(block_in, lambda h, s, pick=pick: (0, 0, pick(h, s))),
            pl.BlockSpec(block_in, lambda h, s, pick=pick: (0, 0, pick(h, s) + steps)),
            pl.BlockSpec(block_out, lambda h, s, pick=pick: (0, 0, pick(h, s))),
        ]
    rows = EXPERTS * CAP
    return pl.pallas_call(
        expert_kernel,
        grid=(2, steps),
        out_shape=jax.ShapeDtypeStruct(arrived.shape, arrived.dtype),
        in_specs=[pl.BlockSpec(memory_space=pltpu.VMEM)] + specs,
        out_specs=pl.BlockSpec(memory_space=pltpu.VMEM),
        scratch_shapes=[
            pltpu.VMEM((rows, width), jnp.bfloat16),
            pltpu.VMEM((rows, width), jnp.float32),
            pltpu.VMEM((EXPERTS * 24, 128), jnp.float32),
        ],
        compiler_params=pltpu.CompilerParams(vmem_limit_bytes=60 * 2**20),
        name="experts",
    )(arrived, own_in, own_in, own_out, peer_in, peer_in, peer_out)


def expert_layer(outgoing, hidden, routes, route_weights, own, peer):
    tokens_here, width = hidden.shape
    vmem = pl.BlockSpec(memory_space=pltpu.VMEM)
    arrived = exchange(outgoing, 1, "exchange_out")
    produced = run_experts(arrived, *own, *peer)
    returned = exchange(produced, 2, "exchange_back")
    mixed = pl.pallas_call(
        combine_kernel,
        out_shape=jax.ShapeDtypeStruct((width, tokens_here), jnp.bfloat16),
        in_specs=[vmem] * 4,
        out_specs=vmem,
        scratch_shapes=[pltpu.VMEM((EXPERTS * 24, 128), jnp.float32)],
        compiler_params=pltpu.CompilerParams(vmem_limit_bytes=40 * 2**20),
        name="combine",
    )(hidden, routes.T, route_weights.T, returned)
    return mixed.T


def shards(
    tokens,
    seg_ids,
    norm_gain,
    query_weight,
    kv_weight,
    out_weight,
    sinks,
    moe_gain,
    routes,
    route_weights,
    expert_in,
    expert_out,
):
    swap = [(c, c + 1 - 2 * (c % 2)) for c in range(lax.axis_size("col"))]
    own_in, own_out = expert_in, jnp.swapaxes(expert_out, 1, 2)
    peer_in, peer_out = (lax.ppermute(w, "col", swap) for w in (own_in, own_out))
    outgoing, hidden, kv_cache = attention_layer(
        tokens,
        seg_ids,
        norm_gain,
        query_weight,
        kv_weight,
        out_weight,
        sinks,
        moe_gain,
        routes,
    )
    mixed = expert_layer(
        outgoing, hidden, routes, route_weights, (own_in, own_out), (peer_in, peer_out)
    )
    return (mixed, kv_cache)


def solution(mesh):
    in_specs = (
        P(("col", "row"), None),
        P(("col", "row")),
        P(),
        P("col", "row"),
        P("col", "row"),
        P("row", "col"),
        P("row"),
        P(),
        P(("col", "row"), None),
        P(("col", "row"), None),
        P(("row", "col"), None, None),
        P(("row", "col"), None, None),
    )
    out_specs = (P(("col", "row"), None), P("col", "row"))
    return jax.shard_map(shards, mesh=mesh, in_specs=in_specs, out_specs=out_specs, check_vma=False)
```

```python
import functools
import math

import jax
import jax.numpy as jnp
import numpy as np
from jax import lax
from jax.experimental import pallas as pl
from jax.experimental.pallas import tpu as pltpu
from jax.sharding import PartitionSpec as P

HD = 64
WIN = 128
EXPERTS = 64
TOP = 4
CAP = 9
SEGS = 16


eps_norm = 1e-05
theta_base = 150000.0
glu_alpha = 1.702
masked_score = -1e30


def rms_scale(widened, gain_vec, width):
    mean_square = jnp.sum(widened * widened, axis=-1, keepdims=True) * (1.0 / width)
    return widened * lax.rsqrt(mean_square + eps_norm) * gain_vec


def chip_place():
    row, col = lax.axis_index("row"), lax.axis_index("col")
    return (row // 4) * 2 + (col // 2) % 2, row % 4, col // 4, col % 2


def device_at(x, y, z, core):
    return ((x // 2) * 4 + y, z * 4 + (x % 2) * 2 + core)


def expert_at(x, y, z):
    return ((x // 2) * 4 + y) * 8 + z * 2 + x % 2


def hop_order():
    every = [
        (dx, (t + dx) % 4, (t // 4 + dx) % 4) for t in range(16) for dx in (1, 3, 2, 0)
    ]
    return [[v for v in every if sum(v) % 2 == odd] for odd in range(2)]


def described(source, target, sems, number, device):
    return pltpu.make_async_remote_copy(
        src_ref=source,
        dst_ref=target,
        send_sem=sems[0].at[number],
        recv_sem=sems[1].at[number],
        device_id=device,
        device_id_type=pl.DeviceIdType.MESH,
    )


def send(*parts):
    copy = described(*parts)
    copy.start()
    return copy


def greet(devices):
    barrier = pltpu.get_barrier_semaphore()
    for device in devices:
        pl.semaphore_signal(
            barrier, inc=1, device_id=device, device_id_type=pl.DeviceIdType.MESH
        )
    pl.semaphore_wait(barrier, len(devices))


class Ring:
    def __init__(self, own, place, device, sems, first):
        self.place, self.device, self.sems, self.first = place, device, sems, first
        self.sent = [
            self.pass_on(0, own(0), 0, 0, 1),
            self.pass_on(1, own(1), 0, 1, 1),
            self.pass_on(2, own(1), 0, 1, 3),
            self.pass_on(3, own(0), 0, 0, 3),
        ]

    def pass_on(self, number, source, owner, half, to):
        return send(
            source, self.place(owner, half), self.sems, self.first + number, self.device(to)
        )

    def take_left(self):
        self.sent[0].wait_recv()
        self.sent.append(self.pass_on(4, self.place(3, 0), 3, 0, 1))
        self.sent[1].wait_recv()

    def take_right(self):
        self.sent[2].wait_recv()
        self.sent.append(self.pass_on(5, self.place(1, 1), 1, 1, 3))
        self.sent[3].wait_recv()

    def take_far(self):
        self.sent[4].wait_recv()
        self.sent[5].wait_recv()

    def close(self):
        for copy in self.sent:
            copy.wait_send()


SHARD_CUT = 96
QUERY_LANES = 8 * HD
PROJ_LANES = QUERY_LANES + 2 * HD


def front_kernel(
    width,
    share,
    xt_ref,
    gain_ref,
    seg_ref,
    freq_ref,
    shard_ref,
    routes_ref,
    out_ref,
    hidden_ref,
    kv_out,
    x_ref,
    w_ref,
    window_ref,
    cos_ref,
    sin_ref,
    pos_ref,
    query_ref,
    kv_ref,
    sum_ref,
    far_ref,
    parts_ref,
    last_ref,
    send_sem,
    recv_sem,
    own_sem,
):
    x, y, z, core = chip_place()
    sems = (send_sem, recv_sem)
    side = x // 2
    run = lax.axis_index("col") * 2 + side
    runs = 2 * lax.axis_size("col")
    shard_rows = shard_ref.shape[0]
    blocks, rows, padded = x_ref.shape
    every = blocks * rows

    def at(first, second):
        return (
            (x + first * core + second * (1 - core)) % 4,
            (z + first * (1 - core) + second * core) % 4,
        )

    def chip(first, second):
        there_x, there_z = at(first, second)
        return device_at(there_x, y, there_z, core)

    def run_device(steps):
        there = (run + steps + runs) % runs
        return ((there % 2) * 4 + y, there // 2)

    def y_device(steps):
        return device_at(x, (y + steps) % 4, z, core)

    sister = device_at(x, y, z, 1 - core)
    partner = device_at((x + 2) % 4, y, z, core)
    greet(
        [y_device(s) for s in (1, 2, 3)]
        + [chip(s, 0) for s in (1, 3)]
        + [chip(0, s) for s in (1, 3)]
        + [sister, partner]
        + [run_device(s) for s in (1, 2, 3, 4, -1, -2, -3, -4)]
    )
    own_seg = pltpu.make_async_copy(seg_ref, window_ref.at[0, y], own_sem.at[0])
    own_seg.start()
    seg_sent = [
        send(seg_ref, window_ref.at[0, y], sems, n, y_device(s)) for n, s in enumerate((1, 2, 3))
    ]

    class Stream:
        def __init__(self, first_sem):
            self.first_sem = first_sem
            self.to_sister, self.rings = [], {}
            self.own = pltpu.make_async_copy(
                self.shard(pl.ds(0, shard_rows)),
                self.place(0, 0, pl.ds(0, shard_rows)),
                own_sem.at[1],
            )
            self.own.start()
            self.along = Ring(
                self.own_half,
                lambda o, h: self.half(o, 0, h),
                lambda s: chip(s, 0),
                sems,
                first_sem,
            )
            self.across(0)

        def shard(self, rows_here):
            return shard_ref.at[rows_here]

        def place(self, first, second, rows_here):
            there_x, there_z = at(first, second)
            slot = there_z * 4 + (there_x % 2) * 2 + core
            start = pl.multiple_of(slot * shard_rows + rows_here.start, 16)
            return w_ref.at[there_x // 2, pl.ds(start, rows_here.size)]

        def cut(self, half):
            if half == 0:
                return pl.ds(0, SHARD_CUT)
            return pl.ds(SHARD_CUT, shard_rows - SHARD_CUT)

        def own_half(self, half):
            return self.shard(self.cut(half))

        def half(self, first, second, half):
            return self.place(first, second, self.cut(half))

        def across(self, owner):
            own = self.own_half if owner == 0 else (lambda h: self.half(owner, 0, h))
            self.rings[owner] = Ring(
                own,
                lambda o, h: self.half(owner, o, h),
                lambda s: chip(0, s),
                sems,
                self.first_sem + 6 + 6 * len(self.rings),
            )
            self.hand_over(owner, 0)

        def hand_over(self, first, second):
            place = self.place(first, second, pl.ds(0, shard_rows))
            own = (first, second) == (0, 0)
            source = self.shard(pl.ds(0, shard_rows)) if own else place
            number = self.first_sem + 30 + len(self.to_sister)
            self.to_sister.append(send(source, place, sems, number, sister))

        def near(self, owner):
            self.rings[owner].take_left()
            self.hand_over(owner, 3)
            self.rings[owner].take_right()
            self.hand_over(owner, 1)

        def far(self, owner):
            self.rings[owner].take_far()
            self.hand_over(owner, 2)

        def arrived(self):
            self.own.wait()
            for copy in self.to_sister:
                copy.wait_recv()

        def close(self):
            for ring in [self.along] + list(self.rings.values()):
                ring.close()
            for copy in self.to_sister:
                copy.wait_send()

    proj = Stream(20)

    raw = xt_ref[...].astype(jnp.float32).T
    normed = rms_scale(raw, gain_ref[0:1, :], width)
    gap = jnp.zeros((rows, shard_rows - share), jnp.float32)
    x_ref[y] = jnp.concatenate(
        [piece for i in range(0, width, share) for piece in (normed[:, i : i + share], gap)],
        axis=1,
    ).astype(jnp.bfloat16)

    own_seg.wait()
    for copy in seg_sent:
        copy.wait_recv()
    seg_on = [
        send(window_ref.at[0], window_ref.at[s], sems, 2 + s, run_device(s)) for s in (1, 2, 3, 4)
    ]
    half_rows = rows // 2
    upper, lower = pl.ds(0, half_rows), pl.ds(half_rows, half_rows)
    x_place = lambda o, h: x_ref.at[(y + o) % 4, lower if h else upper]
    tokens_ring = Ring(lambda h: x_place(0, h), x_place, y_device, sems, 7)

    proj.along.take_left()
    proj.across(3)
    proj.along.take_right()
    proj.across(1)
    proj.rings[0].take_left()
    proj.hand_over(0, 3)
    proj.rings[0].take_right()
    proj.hand_over(0, 1)
    tokens_ring.take_left()
    tokens_ring.take_right()
    proj.along.take_far()
    proj.across(2)
    proj.near(3)
    for copy in seg_on:
        copy.wait_recv()
    fill_tables(run, window_ref, freq_ref, cos_ref, sin_ref, pos_ref)
    proj.near(1)
    proj.near(2)
    for owner in (0, 3, 1, 2):
        proj.far(owner)
    tokens_ring.take_far()
    proj.arrived()

    cosine, sine = cos_ref[...], sin_ref[...]
    lane = lax.broadcasted_iota(jnp.int32, cosine.shape, 1)

    edges = []

    def project(h):
        mixed_kv = jnp.dot(
            x_ref[...].reshape(every, padded),
            w_ref[h, :, :PROJ_LANES],
            preferred_element_type=jnp.float32,
        )
        kv = mixed_kv[:, QUERY_LANES:]
        kv = jnp.where(lane < HD, turned(kv, cosine, sine), kv)
        kv_ref[h, pl.ds(rows, every), :] = kv.astype(jnp.bfloat16)
        edges.append(
            send(
                kv_ref.at[h, pl.ds(every, rows)],
                kv_ref.at[h, pl.ds(0, rows)],
                sems,
                66 + h,
                run_device(1),
            )
        )
        for k in range(0, QUERY_LANES, 128):
            tile = turned(mixed_kv[:, k : k + 128], cosine, sine) * HD**-0.5
            query_ref[:, h * QUERY_LANES + k : h * QUERY_LANES + k + 128] = tile.astype(
                jnp.bfloat16
            )

    project(0)
    project(1)
    mine = pl.ds(pl.multiple_of(side * every, every), every)
    cache_there = send(
        kv_ref.at[1 - side, pl.ds(rows, every)], kv_out.at[mine], sems, 14, partner
    )
    cache_here = pltpu.make_async_copy(
        kv_ref.at[side, pl.ds(rows, every)], kv_out.at[mine], own_sem.at[3]
    )
    cache_here.start()
    for edge in edges:
        edge.wait_recv()
    distance = (
        rows
        + lax.broadcasted_iota(jnp.int32, (rows, 2 * rows), 0)
        - lax.broadcasted_iota(jnp.int32, (rows, 2 * rows), 1)
    ).astype(jnp.float32)

    right, left = y_device(1), y_device(3)
    far_a = (sum_ref.at[0, upper], far_ref.at[0], sems, 15, right)
    far_b = (sum_ref.at[0, lower], far_ref.at[1], sems, 16, left)
    right_b = (sum_ref.at[1, lower], parts_ref.at[0, lower], sems, 17, right)
    left_a = (sum_ref.at[2, upper], parts_ref.at[1, upper], sems, 18, left)
    right_a = (sum_ref.at[1, upper], parts_ref.at[0, upper], sems, 19, right)
    left_b = (sum_ref.at[2, lower], parts_ref.at[1, lower], sems, 13, left)

    def one_block(step, carry):
        block = (y + 10 - step + (step // 2) * (7 - 2 * step)) % 4
        here = pl.ds(pl.multiple_of(block * rows, rows), rows)
        sum_ref[step] = block_sum(
            here,
            pl.ds(pl.multiple_of(block * rows, rows), 2 * rows),
            distance,
            pos_ref,
            query_ref,
            kv_ref,
            w_ref,
        ).astype(jnp.bfloat16)

        @pl.when(step == 0)
        def _():
            send(*far_a)
            send(*far_b)

        @pl.when(step == 1)
        def _():
            send(*right_b)

        @pl.when(step == 2)
        def _():
            send(*left_a)

        return carry

    lax.fori_loop(0, blocks, one_block, 0)
    far_a, far_b, right_b, left_a = (described(*c) for c in (far_a, far_b, right_b, left_a))
    far_a.wait_recv()
    sum_ref[1, upper] = (
        sum_ref[1, upper].astype(jnp.float32) + far_ref[0].astype(jnp.float32)
    ).astype(jnp.bfloat16)
    right_a = send(*right_a)
    far_b.wait_recv()
    sum_ref[2, lower] = (
        sum_ref[2, lower].astype(jnp.float32) + far_ref[1].astype(jnp.float32)
    ).astype(jnp.bfloat16)
    left_b = send(*left_b)
    proj.close()
    tokens_ring.close()
    for copy in seg_sent + seg_on + edges + [far_a, far_b]:
        copy.wait_send()
    total = sum_ref[blocks - 1].astype(jnp.float32)
    hit, rank = slot_grid(routes_ref[...], rows)
    first, last = by_slot(hit, rank, jnp.ones_like(hit))
    for copy in (right_b, left_a, right_a, left_b, cache_there, cache_here):
        copy.wait()
    total = total + parts_ref[0].astype(jnp.float32) + parts_ref[1].astype(jnp.float32)
    hidden = jnp.concatenate(
        [total[:, i : i + share] for i in range(0, padded, shard_rows)], axis=1
    )
    hidden = hidden + xt_ref[...].astype(jnp.float32).T
    hidden_ref[...] = hidden
    moe_in = rms_scale(hidden, gain_ref[1:2, :], width).astype(jnp.bfloat16)
    first, last = first.astype(jnp.bfloat16), last.astype(jnp.bfloat16)
    tiles = tiles_of(width)
    for k, start, wide in tiles:
        piece = moe_in[:, start : start + wide]
        pack_message(
            out_ref,
            last_ref,
            jnp.dot(first, piece, preferred_element_type=jnp.float32),
            jnp.dot(last, piece, preferred_element_type=jnp.float32),
            k,
        )
    finish_message(out_ref, last_ref, len(tiles))


def block_sum(here, near, distance, pos_ref, query_ref, kv_ref, w_ref):
    rows = distance.shape[0]
    heads = QUERY_LANES // HD
    position = pos_ref[here, :]
    position = jnp.concatenate([position, position], axis=1)
    allowed = (distance >= 0) & (distance < WIN) & (distance <= position)
    allowed = jnp.concatenate([allowed.astype(jnp.float32)] * heads, axis=0) > 0.5
    total = None
    for h in range(2):
        keys = kv_ref[h, near, :]
        values = jnp.where(
            lax.broadcasted_iota(jnp.int32, keys.shape, 1) < HD,
            pltpu.roll(keys.astype(jnp.float32), HD, 1),
            1.0,
        ).astype(jnp.bfloat16)
        query = query_ref[here, h * QUERY_LANES : (h + 1) * QUERY_LANES]
        query = jnp.concatenate([query[:, n * HD : (n + 1) * HD] for n in range(heads)], axis=0)
        scores = lax.dot_general(
            query,
            keys[:, :HD],
            (((1,), (1,)), ((), ())),
            preferred_element_type=jnp.float32,
        )
        scores = jnp.where(allowed, scores, masked_score)
        sink_rows = w_ref[h, 176:192, 0:128].astype(jnp.float32)
        sink_row = jnp.sum(sink_rows[4:8], axis=0, keepdims=True)
        sink = jnp.concatenate(
            [jnp.broadcast_to(sink_row[:, n : n + 1], (rows, 1)) for n in range(heads)], axis=0
        )
        ceiling = jnp.maximum(jnp.max(scores, axis=1, keepdims=True), sink)
        expo = jnp.exp(scores - ceiling).astype(jnp.bfloat16)
        mass = jnp.dot(expo, values, preferred_element_type=jnp.float32)
        seen = mass[:, :HD] / (mass[:, HD : HD + 1] + jnp.exp(sink - ceiling))
        seen = jnp.concatenate(
            [seen[n * rows : (n + 1) * rows] for n in range(heads)], axis=1
        ).astype(jnp.bfloat16)
        part = lax.dot_general(
            seen,
            w_ref[h, :, PROJ_LANES:],
            (((1,), (1,)), ((), ())),
            preferred_element_type=jnp.float32,
        )
        total = part if total is None else total + part
    return total


def circle(angle):
    quarter = jnp.floor(angle * (2.0 / math.pi) + 0.5)
    rest = angle - quarter * 1.5703125
    rest = rest - quarter * 4.837512969970703125e-4
    rest = rest - quarter * 7.54978995489188216e-8
    square = rest * rest
    low = rest + rest * square * (
        -1.6666654611e-1 + square * (8.3321608736e-3 - square * 1.9515295891e-4)
    )
    high = (1.0 - 0.5 * square) + square * square * (
        4.166664568298827e-2 + square * (-1.388731625493765e-3 + square * 2.443315711809948e-5)
    )
    turn = quarter.astype(jnp.int32) % 4
    odd = turn % 2 == 1
    sine, cosine = jnp.where(odd, high, low), jnp.where(odd, low, high)
    return (
        jnp.where((turn == 1) | (turn == 2), -cosine, cosine),
        jnp.where(turn >= 2, -sine, sine),
    )


def fill_tables(run, window_ref, freq_ref, cos_ref, sin_ref, pos_ref):
    span, parts, _, lanes = window_ref.shape
    ids = [
        jnp.where(run - s >= 0, window_ref[s].reshape(parts * 8, lanes), -1).astype(jnp.float32)
        for s in range(span)
    ]
    ids = jnp.concatenate(ids, axis=0)
    fewer = [
        jnp.sum((ids < float(s)).astype(jnp.float32), keepdims=True) * 0.125 for s in range(SEGS)
    ]
    lane = lax.broadcasted_iota(jnp.int32, (lanes, lanes), 1)
    row = lax.broadcasted_iota(jnp.int32, (lanes, lanes), 0).astype(jnp.float32)
    for part in range(parts):
        own = window_ref[0, part].astype(jnp.float32)
        own = jnp.broadcast_to(own[0:1, :], (lanes, lanes)).T
        start = jnp.zeros((lanes, lanes), jnp.float32)
        for s in range(SEGS):
            start = jnp.where(own == float(s), fewer[s], start)
        position = row + float((span - 1) * parts * lanes + part * lanes) - start
        angle = position * freq_ref[...]
        cosine, sine = circle(angle)
        here = pl.ds(part * lanes, lanes)
        cos_ref[here, :] = cosine
        sin_ref[here, :] = jnp.where(lane % HD < HD // 2, -sine, sine)
        pos_ref[here, :] = position


def turned(tile, cosine, sine):
    lane = lax.broadcasted_iota(jnp.int32, tile.shape, 1)
    other = jnp.where(
        lane % HD < HD // 2, pltpu.roll(tile, 128 - HD // 2, 1), pltpu.roll(tile, HD // 2, 1)
    )
    return tile * cosine + other * sine


def attention_layer(
    tokens, seg_ids, norm_gain, query_weight, kv_weight, out_weight, sinks, moe_gain, routes
):
    rows, width = tokens.shape
    col_count = lax.axis_size("col")
    share = query_weight.shape[0]
    padded_share = -(-share // 16) * 16
    extra = padded_share - share
    padded = padded_share * col_count
    gains = jnp.stack([norm_gain, moe_gain])
    shard = jnp.concatenate([query_weight, kv_weight, out_weight.T], axis=1)
    rest, sink_terms = sinks, []
    for _ in range(3):
        term = lax.reduce_precision(rest, 8, 7)
        sink_terms.append(term.astype(jnp.bfloat16))
        rest = rest - term
    sink_terms = jnp.pad(
        jnp.stack(sink_terms), ((0, extra - 3), (0, shard.shape[1] - sinks.shape[0]))
    )
    shard = jnp.concatenate([shard, sink_terms], axis=0)
    seg = jnp.broadcast_to(seg_ids[None, :], (8, rows))
    frequency = jnp.asarray(
        np.exp((np.arange(128) % (HD // 2)) * (-2.0 * math.log(theta_base) / HD))[None, :],
        jnp.float32,
    )
    vmem = pl.BlockSpec(memory_space=pltpu.VMEM)
    hbm = pl.BlockSpec(memory_space=pl.ANY)
    bf16, f32 = jnp.bfloat16, jnp.float32
    sem = pltpu.SemaphoreType.DMA
    return pl.pallas_call(
        functools.partial(front_kernel, width, share),
        out_shape=(
            jax.ShapeDtypeStruct((EXPERTS, -(-width // 128) + 3, 8, 128), bf16),
            jax.ShapeDtypeStruct((rows, width), f32),
            jax.ShapeDtypeStruct((8 * rows, 2 * HD), bf16),
        ),
        in_specs=[vmem, vmem, hbm, vmem, hbm, vmem],
        out_specs=(vmem, vmem, hbm),
        scratch_shapes=[
            pltpu.VMEM((4, rows, padded), bf16),
            pltpu.VMEM((2, padded, shard.shape[1]), bf16),
            pltpu.VMEM((5, 4, 8, rows), jnp.int32),
            pltpu.VMEM((4 * rows, 128), f32),
            pltpu.VMEM((4 * rows, 128), f32),
            pltpu.VMEM((4 * rows, 128), f32),
            pltpu.VMEM((4 * rows, 2 * QUERY_LANES), bf16),
            pltpu.VMEM((2, 5 * rows, 2 * HD), bf16),
            pltpu.VMEM((4, rows, padded), bf16),
            pltpu.VMEM((2, rows // 2, padded), bf16),
            pltpu.VMEM((2, rows, padded), bf16),
            pltpu.VMEM((EXPERTS * 24, 128), f32),
            sem((68,)),
            sem((68,)),
            sem((4,)),
        ],
        compiler_params=pltpu.CompilerParams(
            collective_id=3, has_side_effects=True, vmem_limit_bytes=58 * 2**20
        ),
        name="front",
    )(tokens.T, gains, seg, frequency, shard, routes.T)


def slot_grid(routes_t, tokens_here):
    expert_ids = lax.broadcasted_iota(jnp.int32, (EXPERTS, tokens_here), 0)
    hit = jnp.zeros((EXPERTS, tokens_here), jnp.float32)
    for j in range(TOP):
        hit = hit + (routes_t[j : j + 1, :] == expert_ids).astype(jnp.float32)
    earlier = (
        lax.broadcasted_iota(jnp.int32, (tokens_here, tokens_here), 0)
        < lax.broadcasted_iota(jnp.int32, (tokens_here, tokens_here), 1)
    ).astype(jnp.bfloat16)
    rank = jnp.dot(hit.astype(jnp.bfloat16), earlier, preferred_element_type=jnp.float32)
    return hit, rank


def by_slot(hit, rank, amount):
    tokens_here = hit.shape[1]
    slot_ids = lax.broadcasted_iota(jnp.int32, (EXPERTS, 8, tokens_here), 1).astype(jnp.float32)
    first = jnp.where(
        (hit[:, None, :] > 0.5) & (rank[:, None, :] == slot_ids), amount[:, None, :], 0.0
    ).reshape(EXPERTS * 8, tokens_here)
    last = jnp.where((hit > 0.5) & (rank == 8.0), amount, 0.0)
    return first, last


def tiles_of(width):
    return [(k, k * 128, min(128, width - k * 128)) for k in range(-(-width // 128))]


def widen(tile):
    short = 128 - tile.shape[1]
    if short:
        tile = jnp.concatenate([tile, jnp.zeros((tile.shape[0], short), tile.dtype)], axis=1)
    return tile


def pack_message(out_ref, last_ref, tile_first, tile_last, k):
    count = out_ref.shape[0]
    out_ref[:, k] = widen(tile_first).reshape(count, 8, 128).astype(jnp.bfloat16)
    last_ref[pl.ds(k, count, stride=24), :] = widen(tile_last)


def finish_message(out_ref, last_ref, tile_count):
    count = out_ref.shape[0]
    for k in range(tile_count, 24):
        last_ref[pl.ds(k, count, stride=24), :] = jnp.zeros((count, 128), jnp.float32)
    out_ref[:, tile_count:] = last_ref[...].reshape(count, 3, 8, 128).astype(jnp.bfloat16)


def unpack_last(in_ref, last_ref, tile_count):
    count = in_ref.shape[0]
    last_ref[...] = in_ref[:, tile_count:].astype(jnp.float32).reshape(count * 24, 128)


def unpack_tile(in_ref, last_ref, k):
    count = in_ref.shape[0]
    first = in_ref[:, k].astype(jnp.float32).reshape(count * 8, 128)
    last = last_ref[pl.ds(k, count, stride=24), :]
    return jnp.concatenate([first, last], axis=0).astype(jnp.bfloat16)


def combine_kernel(hidden_ref, routes_ref, weights_ref, in_ref, out_ref, last_ref):
    routes_t, weights_t = routes_ref[...], weights_ref[...]
    tokens_here = routes_t.shape[1]
    hit, rank = slot_grid(routes_t, tokens_here)
    expert_ids = lax.broadcasted_iota(jnp.int32, (EXPERTS, tokens_here), 0)
    amount = jnp.zeros((EXPERTS, tokens_here), jnp.float32)
    for j in range(TOP):
        amount = amount + jnp.where(
            routes_t[j : j + 1, :] == expert_ids, weights_t[j : j + 1, :], 0.0
        )
    mix = jnp.concatenate(by_slot(hit, rank, amount), axis=0).T
    mix_high = mix.astype(jnp.bfloat16)
    mix_low = (mix - mix_high.astype(jnp.float32)).astype(jnp.bfloat16)
    tiles = tiles_of(out_ref.shape[0])
    unpack_last(in_ref, last_ref, len(tiles))
    for k, start, width in tiles:
        rows = unpack_tile(in_ref, last_ref, k)
        total = jnp.dot(mix_high, rows, preferred_element_type=jnp.float32) + jnp.dot(
            mix_low, rows, preferred_element_type=jnp.float32
        )
        here = slice(start, start + width)
        total = (widen(hidden_ref[:, here]) + total).T
        out_ref[here, :] = total[:width].astype(jnp.bfloat16)


def expert_kernel(
    out_msgs,
    own_in,
    own_out,
    peer_in,
    peer_out,
    back_msgs,
    in_ref,
    out_ref,
    up_ref,
    down_ref,
    rows_ref,
    total_ref,
    last_ref,
    send_sem,
    recv_sem,
    back_send_sem,
    back_recv_sem,
    own_sem,
):
    x, y, z, core = chip_place()
    me = expert_at(x, y, z)
    groups = hop_order()
    order = groups[0] + groups[1]
    in_group = len(groups[0])
    width = total_ref.shape[1]
    tiles = tiles_of(width)
    chunk = 256
    steps = down_ref.shape[2] // chunk

    def there(offset, sign):
        return tuple((here + sign * step + 4) % 4 for here, step in zip((x, y, z), offset))

    loads = [
        pltpu.make_async_copy(source.at[0], target, own_sem.at[n])
        for n, (source, target) in enumerate(
            (
                (own_in, up_ref.at[0]),
                (own_out, down_ref.at[0]),
                (peer_in, up_ref.at[1]),
                (peer_out, down_ref.at[1]),
            )
        )
    ]
    greet([device_at(*there(v, 1), core) for v in order if v != (0, 0, 0)])
    arriving, going_back = [], []
    for number, offset in enumerate(order):
        if offset == (0, 0, 0):
            copy = pltpu.make_async_copy(out_msgs.at[me], in_ref.at[number], own_sem.at[4])
            copy.start()
        else:
            target = there(offset, 1)
            copy = send(
                out_msgs.at[expert_at(*target)],
                in_ref.at[number],
                (send_sem, recv_sem),
                number,
                device_at(*target, core),
            )
        arriving.append(copy)
    for load in loads:
        load.start()

    for group in range(2):
        first = group * in_group
        here = pl.ds(first, in_group)
        for number in range(first, first + in_group):
            if order[number] == (0, 0, 0):
                arriving[number].wait()
            else:
                arriving[number].wait_recv()
        unpack_last(in_ref.at[here], last_ref, len(tiles))
        for k, start, wide in tiles:
            rows_ref[:, start : start + wide] = unpack_tile(in_ref.at[here], last_ref, k)[:, :wide]
        if group == 0:
            for load in loads:
                load.wait()
        total_ref[...] = jnp.zeros_like(total_ref)

        def one_step(step, carry):
            half, lane = step // steps, (step % steps) * chunk
            gate_lanes = pl.ds(pl.multiple_of(lane, chunk), chunk)
            up_lanes = pl.ds(pl.multiple_of(lane + steps * chunk, chunk), chunk)
            rows = rows_ref[...]
            gate_part = jnp.dot(
                rows, up_ref[half, :, gate_lanes], preferred_element_type=jnp.float32
            )
            up_part = jnp.dot(rows, up_ref[half, :, up_lanes], preferred_element_type=jnp.float32)
            act = (gate_part * jax.nn.sigmoid(glu_alpha * gate_part) * (up_part + 1.0)).astype(
                jnp.bfloat16
            )
            total_ref[...] += lax.dot_general(
                act,
                down_ref[half, :, gate_lanes],
                (((1,), (1,)), ((), ())),
                preferred_element_type=jnp.float32,
            )
            return carry

        lax.fori_loop(0, 2 * steps, one_step, 0)
        for k, start, wide in tiles:
            tile = total_ref[:, start : start + wide]
            pack_message(
                out_ref.at[here], last_ref, tile[: in_group * 8], tile[in_group * 8 :], k
            )
        finish_message(out_ref.at[here], last_ref, len(tiles))
        for number in range(first, first + in_group):
            if order[number] == (0, 0, 0):
                copy = pltpu.make_async_copy(out_ref.at[number], back_msgs.at[me], own_sem.at[5])
                copy.start()
            else:
                copy = send(
                    out_ref.at[number],
                    back_msgs.at[me],
                    (back_send_sem, back_recv_sem),
                    number,
                    device_at(*there(order[number], -1), core),
                )
            going_back.append(copy)
    for number, copy in enumerate(arriving):
        if order[number] != (0, 0, 0):
            copy.wait_send()
    for copy in going_back:
        copy.wait()


def run_experts(outgoing, own_in, own_out, peer_in, peer_out):
    width, hidden_width = own_in.shape[1:]
    hbm = pl.BlockSpec(memory_space=pl.ANY)
    rows = EXPERTS * CAP // 2
    sem = pltpu.SemaphoreType.DMA
    return pl.pallas_call(
        expert_kernel,
        out_shape=jax.ShapeDtypeStruct(outgoing.shape, outgoing.dtype),
        in_specs=[hbm] * 5,
        out_specs=hbm,
        scratch_shapes=[
            pltpu.VMEM(outgoing.shape, jnp.bfloat16),
            pltpu.VMEM(outgoing.shape, jnp.bfloat16),
            pltpu.VMEM((2, width, hidden_width), jnp.bfloat16),
            pltpu.VMEM((2, width, hidden_width // 2), jnp.bfloat16),
            pltpu.VMEM((rows, width), jnp.bfloat16),
            pltpu.VMEM((rows, width), jnp.float32),
            pltpu.VMEM((EXPERTS // 2 * 24, 128), jnp.float32),
        ]
        + [sem((EXPERTS,))] * 4
        + [sem((6,))],
        compiler_params=pltpu.CompilerParams(
            collective_id=1, has_side_effects=True, vmem_limit_bytes=60 * 2**20
        ),
        name="experts",
    )(outgoing, own_in, own_out, peer_in, peer_out)


def expert_layer(outgoing, hidden, routes, route_weights, own, peer):
    tokens_here, width = hidden.shape
    vmem = pl.BlockSpec(memory_space=pltpu.VMEM)
    returned = run_experts(outgoing, *own, *peer)
    mixed = pl.pallas_call(
        combine_kernel,
        out_shape=jax.ShapeDtypeStruct((width, tokens_here), jnp.bfloat16),
        in_specs=[vmem] * 4,
        out_specs=vmem,
        scratch_shapes=[pltpu.VMEM((EXPERTS * 24, 128), jnp.float32)],
        compiler_params=pltpu.CompilerParams(vmem_limit_bytes=40 * 2**20),
        name="combine",
    )(hidden, routes.T, route_weights.T, returned)
    return mixed.T


def shards(
    tokens,
    seg_ids,
    norm_gain,
    query_weight,
    kv_weight,
    out_weight,
    sinks,
    moe_gain,
    routes,
    route_weights,
    expert_in,
    expert_out,
):
    swap = [(c, c + 1 - 2 * (c % 2)) for c in range(lax.axis_size("col"))]
    own_in, own_out = expert_in, jnp.swapaxes(expert_out, 1, 2)
    peer_in, peer_out = (lax.ppermute(w, "col", swap) for w in (own_in, own_out))
    outgoing, hidden, kv_cache = attention_layer(
        tokens,
        seg_ids,
        norm_gain,
        query_weight,
        kv_weight,
        out_weight,
        sinks,
        moe_gain,
        routes,
    )
    mixed = expert_layer(
        outgoing, hidden, routes, route_weights, (own_in, own_out), (peer_in, peer_out)
    )
    return (mixed, kv_cache)


def solution(mesh):
    in_specs = (
        P(("col", "row"), None),
        P(("col", "row")),
        P(),
        P("col", "row"),
        P("col", "row"),
        P("row", "col"),
        P("row"),
        P(),
        P(("col", "row"), None),
        P(("col", "row"), None),
        P(("row", "col"), None, None),
        P(("row", "col"), None, None),
    )
    out_specs = (P(("col", "row"), None), P("col", "row"))
    return jax.shard_map(shards, mesh=mesh, in_specs=in_specs, out_specs=out_specs, check_vma=False)
```
